32 devices in a mesh: planes: 16 (over z, y, x), elem: 2 (over core).
Axes of the slice: x: 2, y: 2, z: 4, core: 2. Of those that a mesh axis runs over, the one named last changes fastest.
Arguments:
- velocity: float32 [3, 256, 20736], P(None, 'planes', 'elem'), may hold values from -6 to 6
- geometry: float32 [4, 20736], P(None, 'elem'), may hold values from -1.5 to 1.5
- element_kind: int32 [256], P('elem'), may hold values from 0 to 1
- element_scale: float32 [256], P('elem'), may hold values from 0.5 to 2
- dirichlet: int32 [2, 9, 256], P(None, None, 'elem'), may hold values 0 or 1
- schur_stiffness: float32 [2, 36, 36], replicated, may hold values from -0.2 to 8.5, as said below
- schur_mass: float32 [2, 36, 36], replicated, may hold values from -0.1 to 4.5, as said below
- lift: float32 [2, 36, 81], replicated, may hold values from -0.625 to 0.625
- recover: float32 [2, 81, 36], replicated, may hold values from -1 to 1
Outputs:
- new_velocity: float32 [3, 256, 20736], P(None, 'planes', 'elem')
The draws below stay inside these ranges and needn't reach their ends.
Inputs may be any that keep to these rules, and one draw needn't show every extreme that they name: `schur_stiffness`: each of the two matrices is symmetric and positive definite. `schur_mass`: each of the two matrices is symmetric and positive definite.
All inputs are finite; a program needn't handle non-finite values. No bound on the sum of `dirichlet` on one device may be relied on, other than what follows from the above.
Results may differ from the reference program's by a relative error of at most 0.0001.
Values sent between devices are 32-bit elements; how exact they have to be, the bound alone decides.
A program may use at most 128 MiB of HBM per device.

```python
import math
import jax
import jax.numpy as jnp
import numpy as np
from jax import lax

PLANES = 256
QUAD = 9
COLUMN_ELEMS = 32
CG_STEPS = 4
ELEMS = 256
NODES = 20736


def symmetric_dominant(key, off_scale, lo, hi):
    size = 4 * QUAD
    keys = jax.random.split(key, 2)
    upper = jnp.triu(jax.random.uniform(keys[0], (2, size, size), jnp.float32, -off_scale, off_scale), 1)
    off_part = upper + jnp.swapaxes(upper, 1, 2)
    rowsum = jnp.sum(jnp.abs(off_part), axis=2)
    extra = jax.random.uniform(keys[1], (2, size), jnp.float32, lo, hi)
    return off_part + jnp.eye(size, dtype=jnp.float32)[None] * (rowsum + extra)[:, :, None]


def draw_schur_stiffness(key, part):
    return symmetric_dominant(jax.random.fold_in(key, 11), 0.2, 0.5, 1.5)


def draw_schur_mass(key, part):
    return symmetric_dominant(jax.random.fold_in(key, 23), 0.1, 0.5, 1.0)


def place_ends(result, stream_key, low, largest):
    index_at = [jax.random.randint(jax.random.fold_in(stream_key, axis), (), 0, length) for axis, length in enumerate(result.shape)]
    longest = result.shape.index(max(result.shape))
    neighbour = index_at[:longest] + [(index_at[longest] + 1) % result.shape[longest]] + index_at[longest + 1:]
    return result.at[tuple(index_at)].set(low).at[tuple(neighbour)].set(largest)


def block_levels(key, dims, cuts, least, largest):
    def one(position, blocks):
        steps = jax.random.uniform(jax.random.fold_in(jax.random.fold_in(key, 6), position), (blocks,), jnp.float32, least / len(cuts), largest / len(cuts))
        return jnp.repeat(jnp.exp(steps), dims[position] // blocks).reshape((-1,) + (1,) * (len(dims) - position - 1))

    gain = one(*cuts[0])
    for cut in cuts[1:]:
        gain = gain * one(*cut)
    return gain


def centred(stream_key, extent, deviation, bound, shards=(), kind=jnp.bfloat16):
    factor_of = block_levels(stream_key, extent, shards, -0.22, 0.18) if shards else 1.0
    result = jax.random.normal(stream_key, extent, jnp.float32) * deviation * factor_of
    return jnp.minimum(jnp.maximum(result, -bound), bound).astype(kind)


def setup_inputs(seed: int = 0) -> dict:
    streams_of = jax.random.split(jax.random.key(seed), 10)
    velocity = centred(streams_of[0], (3, PLANES, NODES), 1.0, 6.0, ((1, 16), (2, 2)), jnp.float32)
    geometry = jnp.clip(jax.random.uniform(streams_of[1], (4, NODES), jnp.float32, -1.5, 1.5) * block_levels(streams_of[1], (4, NODES), ((1, 2),), -0.4, 0.0), -1.5, 1.5)
    element_kind = place_ends(jax.random.randint(streams_of[2], (ELEMS,), 0, 2), jax.random.fold_in(streams_of[2], 1), 0, 1).astype(jnp.int32)
    element_scale = jnp.clip(jnp.exp(math.log(2.0) - 1.3862944 * jax.random.uniform(streams_of[3], (ELEMS,), jnp.float32) ** block_levels(streams_of[3], (ELEMS,), ((0, 2),), -0.2, 0.2)), 0.5, 2.0)
    dirichlet = place_ends((jax.random.randint(streams_of[4], (2, QUAD, ELEMS), 0, 6) < 1).astype(jnp.int32), jax.random.fold_in(streams_of[4], 1), 0, 1)
    schur_stiffness = draw_schur_stiffness(jax.random.fold_in(streams_of[9], 71), 0)
    schur_mass = draw_schur_mass(jax.random.fold_in(streams_of[9], 71), 0)
    lift = centred(streams_of[7], (2, 4 * QUAD, QUAD * QUAD), (QUAD * QUAD) ** -0.5, 0.625, (), jnp.float32)
    recover = centred(streams_of[8], (2, QUAD * QUAD, 4 * QUAD), (4 * QUAD) ** -0.5, 1.0, (), jnp.float32)
    return {"velocity": velocity, "geometry": geometry, "element_kind": element_kind, "element_scale": element_scale, "dirichlet": dirichlet, "schur_stiffness": schur_stiffness, "schur_mass": schur_mass, "lift": lift, "recover": recover}


HIGHEST = lax.Precision.HIGHEST
SIGMA_COEF = 1.0
BETA_COEF = 0.01
STEP_DT = 0.002


def gauss_derivative(points):
    nodes = -np.cos(np.pi * (2 * np.arange(points) + 1) / (2 * points))
    ident = np.eye(points)
    diffs = nodes[:, None] - nodes[None, :] + ident
    weights = 1.0 / np.prod(diffs, axis=1)
    matrix = (weights[None, :] / weights[:, None]) / diffs
    matrix = matrix * (1.0 - ident)
    return matrix - ident * matrix.sum(axis=1)[:, None]


def kron_tables():
    deriv = gauss_derivative(QUAD)
    identity = np.eye(QUAD)
    return jnp.asarray(np.kron(deriv, identity), jnp.float32), jnp.asarray(np.kron(identity, deriv), jnp.float32)


def synthesize(coef, slope):
    planes = coef.shape[1]
    half = planes // 2
    pairs = coef[:, 1:planes - 1].reshape(coef.shape[0], half - 1, 2, coef.shape[2])
    cosine = pairs[:, :, 0]
    sine = pairs[:, :, 1]
    mean = coef[:, :1]
    top = coef[:, planes - 1:]
    if slope:
        rate = BETA_COEF * jnp.arange(1, half, dtype=jnp.float32)[None, :, None]
        cosine, sine = rate * sine, -rate * cosine
        mean = jnp.zeros_like(mean)
        top = jnp.zeros_like(top)
    real = jnp.concatenate([mean * planes, cosine * (planes / 2), top * planes], axis=1)
    imag = jnp.concatenate([jnp.zeros_like(mean), -sine * (planes / 2), jnp.zeros_like(top)], axis=1)
    return jnp.fft.irfft(lax.complex(real, imag), n=planes, axis=1)


def analyze(field):
    planes = field.shape[1]
    spectrum = jnp.fft.rfft(field, axis=1)
    real = jnp.real(spectrum)
    imag = jnp.imag(spectrum)
    mean = real[:, :1] / planes
    top = real[:, planes // 2:] / planes
    cosine = real[:, 1:planes // 2] * (2.0 / planes)
    sine = -imag[:, 1:planes // 2] * (2.0 / planes)
    pairs = jnp.stack([cosine, sine], axis=2).reshape(field.shape[0], planes - 2, field.shape[2])
    return jnp.concatenate([mean, pairs, top], axis=1)


def advect_block(coef, geo, first, second):
    values = synthesize(coef, False)
    along_z = synthesize(coef, True)
    shaped = values.reshape(3, values.shape[1], -1, QUAD * QUAD)
    along_r = jnp.einsum('cpen,mn->cpem', shaped, first, precision=HIGHEST).reshape(values.shape)
    along_s = jnp.einsum('cpen,mn->cpem', shaped, second, precision=HIGHEST).reshape(values.shape)
    along_x = geo[0] * along_r + geo[1] * along_s
    along_y = geo[2] * along_r + geo[3] * along_s
    advection = values[0] * along_x + values[1] * along_y + values[2] * along_z
    return analyze(advection)


def element_vector(vertical, horizontal):
    right = jnp.concatenate([vertical[:, :, COLUMN_ELEMS:], jnp.zeros_like(vertical[:, :, :COLUMN_ELEMS])], axis=2)
    grid = horizontal.reshape(horizontal.shape[0], horizontal.shape[1], -1, COLUMN_ELEMS)
    top = jnp.concatenate([grid[..., 1:], jnp.zeros_like(grid[..., :1])], axis=3).reshape(horizontal.shape)
    return jnp.concatenate([vertical, right, horizontal, top], axis=0)


def element_apply(vector, lam, second_kind, scale, stiffness, mass):
    flat = vector.reshape(vector.shape[0], -1)
    results = []
    for kind in range(2):
        stiff = jnp.dot(stiffness[kind], flat, precision=HIGHEST).reshape(vector.shape)
        massed = jnp.dot(mass[kind], flat, precision=HIGHEST).reshape(vector.shape)
        results.append(stiff + lam[None, :, None] * massed)
    return scale[None, None, :] * jnp.where(second_kind[None, None, :], results[1], results[0])


def assemble(outputs, free):
    left = outputs[:QUAD]
    right = outputs[QUAD:2 * QUAD]
    bottom = outputs[2 * QUAD:3 * QUAD]
    top = outputs[3 * QUAD:]
    vertical = left + jnp.concatenate([jnp.zeros_like(right[:, :, :COLUMN_ELEMS]), right[:, :, :-COLUMN_ELEMS]], axis=2)
    grid = top.reshape(top.shape[0], top.shape[1], -1, COLUMN_ELEMS)
    shifted = jnp.concatenate([jnp.zeros_like(grid[..., :1]), grid[..., :-1]], axis=3).reshape(bottom.shape)
    horizontal = bottom + shifted
    return vertical * free[0], horizontal * free[1]


def inner(first_pair, second_pair):
    return jnp.sum(first_pair[0] * second_pair[0], axis=(0, 2)) + jnp.sum(first_pair[1] * second_pair[1], axis=(0, 2))


def solve_component(comp, lam, free, second_kind, scale, stiffness, mass, lift, recover):
    planes = comp.shape[0]
    node_values = (SIGMA_COEF * comp).reshape(planes, ELEMS, QUAD * QUAD)
    lifted = jnp.where(second_kind[None, None, :],
                       jnp.einsum('kn,ren->kre', lift[1], node_values, precision=HIGHEST),
                       jnp.einsum('kn,ren->kre', lift[0], node_values, precision=HIGHEST))
    forcing = assemble(lifted, free)
    trace = (jnp.zeros_like(forcing[0]), jnp.zeros_like(forcing[1]))
    residual = forcing
    direction = forcing
    norm_now = inner(residual, residual)
    for sweep in range(CG_STEPS):
        image = assemble(element_apply(element_vector(direction[0], direction[1]), lam, second_kind, scale, stiffness, mass), free)
        alpha = (norm_now / inner(direction, image))[None, :, None]
        trace = (trace[0] + alpha * direction[0], trace[1] + alpha * direction[1])
        residual = (residual[0] - alpha * image[0], residual[1] - alpha * image[1])
        norm_next = inner(residual, residual)
        ratio = (norm_next / norm_now)[None, :, None]
        direction = (residual[0] + ratio * direction[0], residual[1] + ratio * direction[1])
        norm_now = norm_next
    vector = element_vector(trace[0], trace[1])
    recovered = jnp.where(second_kind[None, :, None],
                          jnp.einsum('nl,lre->ren', recover[1], vector, precision=HIGHEST),
                          jnp.einsum('nl,lre->ren', recover[0], vector, precision=HIGHEST))
    weight = SIGMA_COEF / (SIGMA_COEF + lam)
    return comp * weight[:, None] + recovered.reshape(comp.shape)


def reference(velocity, geometry, element_kind, element_scale, dirichlet, schur_stiffness, schur_mass, lift, recover):
    first, second = kron_tables()
    planes = velocity.shape[1]
    columns = ELEMS // COLUMN_ELEMS
    width = COLUMN_ELEMS * QUAD * QUAD
    blocks = velocity.reshape(3, planes, columns, width).transpose(2, 0, 1, 3)
    geo_blocks = geometry.reshape(4, columns, width).transpose(1, 0, 2)
    advected = lax.map(lambda pair: advect_block(pair[0], pair[1], first, second), (blocks, geo_blocks))
    advection_hat = advected.transpose(1, 2, 0, 3).reshape(velocity.shape)
    intermediate = velocity - STEP_DT * advection_hat
    waves = ((jnp.arange(planes, dtype=jnp.int32) + 1) // 2).astype(jnp.float32)
    lam = SIGMA_COEF + (BETA_COEF * waves) ** 2
    free = (1 - dirichlet).astype(jnp.float32)[:, :, None, :]
    second_kind = element_kind == 1
    return lax.map(lambda comp: solve_component(comp, lam, free, second_kind, element_scale,
                                                schur_stiffness, schur_mass, lift, recover), intermediate)
```

```python
import math

import jax
import jax.numpy as jnp
import numpy as np
from jax import lax
from jax.experimental import pallas as pl
from jax.experimental.pallas import tpu as pltpu
from jax.sharding import PartitionSpec as P

PLANES = 256
QUAD = 9
COLUMN_ELEMS = 32
CG_STEPS = 4


HIGHEST = lax.Precision.HIGHEST
SIGMA_COEF = 1.0
BETA_COEF = 0.01
STEP_DT = 0.002


def passed_along(value, axis, steps):
    count = lax.axis_size(axis)
    leading, last = (max(0, -steps), min(count, count - steps))
    return lax.ppermute(value, axis, [(source, source + steps) for source in range(leading, last)])


def gauss_derivative(points):
    nodes = -np.cos(np.pi * (2 * np.arange(points) + 1) / (2 * points))
    ident = np.eye(points)
    diffs = nodes[:, None] - nodes[None, :] + ident
    weights = 1.0 / np.prod(diffs, axis=1)
    matrix = weights[None, :] / weights[:, None] / diffs
    matrix = matrix * (1.0 - ident)
    return matrix - ident * matrix.sum(axis=1)[:, None]


def kron_tables():
    deriv = gauss_derivative(QUAD)
    identity = np.eye(QUAD)
    return (
        jnp.asarray(np.kron(deriv, identity), jnp.float32),
        jnp.asarray(np.kron(identity, deriv), jnp.float32),
    )


def fourier_tables(planes):
    zeta = jnp.arange(planes, dtype=jnp.int32)
    rows = jnp.arange(planes, dtype=jnp.int32)
    waves = (rows + 1) // 2
    phase = waves[None, :] * zeta[:, None] % planes
    angle = 2.0 * math.pi / planes * phase.astype(jnp.float32)
    cosine = jnp.cos(angle)
    sine = jnp.sin(angle)
    odd = (rows % 2 == 1)[None, :]
    first = (rows == 0)[None, :]
    last = (rows == planes - 1)[None, :]
    synth = jnp.where(first, 1.0, jnp.where(odd, cosine, sine))
    rate = BETA_COEF * waves.astype(jnp.float32)[None, :]
    slope = jnp.where(first | last, 0.0, jnp.where(odd, -rate * sine, rate * cosine))
    weight = jnp.where((rows == 0) | (rows == planes - 1), 1.0 / planes, 2.0 / planes).astype(
        jnp.float32
    )
    analysis = synth.T * weight[:, None]
    return (synth, slope, analysis)


def inner(first_pair, second_pair):
    return jnp.sum(first_pair[0] * second_pair[0], axis=(0, 2)) + jnp.sum(
        first_pair[1] * second_pair[1], axis=(0, 2)
    )


def global_total(first_pair, second_pair):
    return lax.psum(inner(first_pair, second_pair), "elem")


def global_squares(pair):
    return lax.psum(inner(pair, pair), "elem")


def assemble(outputs, incoming, free):
    left = outputs[:QUAD]
    right = outputs[QUAD : 2 * QUAD]
    bottom = outputs[2 * QUAD : 3 * QUAD]
    top = outputs[3 * QUAD :]
    vertical = left + jnp.concatenate([incoming, right[:, :, :-COLUMN_ELEMS]], axis=2)
    grid = top.reshape(top.shape[0], top.shape[1], -1, COLUMN_ELEMS)
    shifted = jnp.concatenate([jnp.zeros_like(grid[..., :1]), grid[..., :-1]], axis=3).reshape(
        bottom.shape
    )
    horizontal = bottom + shifted
    return (vertical * free[0], horizontal * free[1])


def plain_device(
    velocity,
    geometry,
    element_kind,
    element_scale,
    dirichlet,
    schur_stiffness,
    schur_mass,
    lift,
    recover,
):
    first, second = kron_tables()
    synth, slope, analysis = fourier_tables(PLANES)
    local_rows = velocity.shape[1]
    node_count = velocity.shape[2]
    share = node_count // lax.axis_size("planes")
    geo_part = lax.dynamic_slice_in_dim(geometry, lax.axis_index("planes") * share, share, 1)

    def transform(table, field):
        return jnp.einsum("zr,crm->czm", table, field, precision=HIGHEST)

    items = lax.all_to_all(velocity, "planes", split_axis=2, concat_axis=1, tiled=True)
    values = transform(synth, items)
    along_z = transform(slope, items)
    shaped = values.reshape(values.shape[:-1] + (-1, QUAD * QUAD))
    along_r = jnp.einsum("...en,mn->...em", shaped, first, precision=HIGHEST).reshape(values.shape)
    along_s = jnp.einsum("...en,mn->...em", shaped, second, precision=HIGHEST).reshape(values.shape)
    along_x = geo_part[0] * along_r + geo_part[1] * along_s
    along_y = geo_part[2] * along_r + geo_part[3] * along_s
    values, along_x, along_y, along_z = (values, along_x, along_y, along_z)
    advection = values[0] * along_x + values[1] * along_y + values[2] * along_z
    advection_hat = jnp.einsum("rz,czm->crm", analysis, advection, precision=HIGHEST)
    returned = lax.all_to_all(advection_hat, "planes", split_axis=1, concat_axis=2, tiled=True)
    intermediate = velocity - STEP_DT * returned
    elem_count = element_kind.shape[0]
    row_count = 3 * local_rows
    waves = (
        (lax.axis_index("planes") * local_rows + jnp.arange(local_rows, dtype=jnp.int32) + 1) // 2
    ).astype(jnp.float32)
    lam = jnp.tile(SIGMA_COEF + (BETA_COEF * waves) ** 2, 3)
    free = (1 - dirichlet).astype(jnp.float32)[:, :, None, :]
    chooser = (element_kind == 1).astype(jnp.float32)

    def element_apply(vector, kinds, scales):
        flat = vector.reshape(vector.shape[0], -1)
        results = []
        for kind in range(2):
            stiff = jnp.dot(schur_stiffness[kind], flat, precision=HIGHEST).reshape(vector.shape)
            massed = jnp.dot(schur_mass[kind], flat, precision=HIGHEST).reshape(vector.shape)
            results.append(stiff + lam[None, :, None] * massed)
        return scales[None, None, :] * jnp.where(kinds[None, None, :] > 0.5, results[1], results[0])

    def element_vector(vertical, horizontal):
        arriving = passed_along(vertical[:, :, :COLUMN_ELEMS], "elem", -1)
        right = jnp.concatenate([vertical[:, :, COLUMN_ELEMS:], arriving], axis=2)
        grid = horizontal.reshape(horizontal.shape[0], horizontal.shape[1], -1, COLUMN_ELEMS)
        top = jnp.concatenate([grid[..., 1:], jnp.zeros_like(grid[..., :1])], axis=3).reshape(
            horizontal.shape
        )
        return jnp.concatenate([vertical, right, horizontal, top], axis=0)

    node_values = (SIGMA_COEF * intermediate).reshape(row_count, elem_count, QUAD * QUAD)
    lifted = jnp.where(
        chooser[None, None, :] > 0.5,
        jnp.einsum("kn,ren->kre", lift[1], node_values, precision=HIGHEST),
        jnp.einsum("kn,ren->kre", lift[0], node_values, precision=HIGHEST),
    )
    lifted_right = passed_along(lifted[QUAD : 2 * QUAD, :, -COLUMN_ELEMS:], "elem", 1)
    forcing = assemble(lifted, lifted_right, free)
    trace = (jnp.zeros_like(forcing[0]), jnp.zeros_like(forcing[1]))
    residual = forcing
    direction = forcing
    norm_now = global_squares(residual)
    for sweep in range(CG_STEPS):
        outputs = element_apply(element_vector(direction[0], direction[1]), chooser, element_scale)
        operator_arriving = passed_along(outputs[QUAD : 2 * QUAD, :, -COLUMN_ELEMS:], "elem", 1)
        image = assemble(outputs, operator_arriving, free)
        alpha = (norm_now / global_total(direction, image))[None, :, None]
        trace = (trace[0] + alpha * direction[0], trace[1] + alpha * direction[1])
        residual = (residual[0] - alpha * image[0], residual[1] - alpha * image[1])
        norm_next = global_squares(residual)
        ratio = (norm_next / norm_now)[None, :, None]
        direction = (residual[0] + ratio * direction[0], residual[1] + ratio * direction[1])
        norm_now = norm_next
    vector = element_vector(trace[0], trace[1])
    recovered = jnp.where(
        chooser[None, :, None] > 0.5,
        jnp.einsum("nl,lre->ren", recover[1], vector, precision=HIGHEST),
        jnp.einsum("nl,lre->ren", recover[0], vector, precision=HIGHEST),
    )
    weight = SIGMA_COEF / (SIGMA_COEF + lam)
    result = (
        intermediate.reshape(row_count, elem_count, QUAD * QUAD) * weight[:, None, None] + recovered
    )
    return result.reshape(velocity.shape)


LANES = 128
SUB = 16
F32 = jnp.float32
BF16 = jnp.bfloat16


def split(value):
    high = value.astype(BF16)
    return high, (value - high.astype(F32)).astype(BF16)


def np_split(value):
    high = np.asarray(value, np.float32).astype(BF16)
    low = (np.asarray(value, np.float64) - high.astype(np.float64)).astype(np.float32).astype(BF16)
    return high, low


def mm(first, second):
    return jnp.dot(first, second, preferred_element_type=F32)


def stacked_weights(weights):
    high, low = split(weights)
    return jnp.concatenate([high, high, low], axis=1)


def stacked_values(values):
    high, low = split(values)
    return jnp.concatenate([high, low, high], axis=0)


def advect_tables(planes):
    zeta = np.arange(planes)
    rows = np.arange(planes)
    waves = (rows + 1) // 2
    angle = 2.0 * np.pi / planes * ((waves[None, :] * zeta[:, None]) % planes)
    odd = (rows % 2 == 1)[None, :]
    first = (rows == 0)[None, :]
    last = (rows == planes - 1)[None, :]
    synth = np.where(first, 1.0, np.where(odd, np.cos(angle), np.sin(angle)))
    rate = BETA_COEF * waves[None, :]
    slope = np.where(first | last, 0.0, np.where(odd, -rate * np.sin(angle), rate * np.cos(angle)))
    weight = np.where((rows == 0) | (rows == planes - 1), 1.0 / planes, 2.0 / planes)
    analysis = synth.T * weight[:, None]
    high, low = np_split(np.concatenate([synth, slope], axis=0))
    forward = np.concatenate([high, high, low], axis=1)
    high, low = np_split(analysis)
    backward = np.concatenate([high, high, low], axis=1)
    points = QUAD * QUAD
    deriv = gauss_derivative(QUAD)
    both = np.zeros((LANES, 2 * LANES))
    both[:points, :points] = np.kron(deriv, np.eye(QUAD)).T
    both[:points, LANES : LANES + points] = np.kron(np.eye(QUAD), deriv).T
    high, low = np_split(both)
    return jnp.asarray(forward), jnp.asarray(backward), jnp.asarray(np.concatenate([high, high, low], axis=0))


def whole_spec(shape):
    return pl.BlockSpec(shape, lambda *_: (0,) * len(shape))


def params():
    return pltpu.CompilerParams(vmem_limit_bytes=60 * 1024 * 1024)


def pack_messages(velocity, count):
    comps, rows, nodes = velocity.shape
    points = QUAD * QUAD
    per = nodes // points // count

    def kernel(src, dst):
        for part in range(count):
            pieces = []
            for local in range(per):
                at = (part * per + local) * points
                pieces.append(src[0, :, at : at + points])
            dst[part, 0] = jnp.concatenate(pieces, axis=0).T

    return pl.pallas_call(
        kernel,
        grid=(comps,),
        in_specs=[pl.BlockSpec((1, rows, nodes), lambda c: (c, 0, 0))],
        out_specs=pl.BlockSpec((count, 1, points, LANES), lambda c: (0, c, 0, 0)),
        out_shape=jax.ShapeDtypeStruct((count, comps, points, LANES), F32),
        compiler_params=params(),
        name="pack_messages",
    )(velocity)


def advect(received, geometry, planes, rows):
    count, comps, points, _ = received.shape
    per = LANES // rows
    pairs = per // 2
    width = 2 * comps * LANES
    forward, backward, deriv = advect_tables(planes)

    def kernel(src, geo, forward_ref, backward_ref, deriv_ref, dst, store):
        def lanes_of(local, comp):
            at = ((local % 2) * comps + comp) * LANES
            return slice(at, at + LANES)

        def arrive(part, carry):
            for comp in range(comps):
                block = jnp.concatenate([src[part, comp], jnp.zeros((LANES - points, LANES), F32)], axis=0).T
                for local in range(per):
                    store[local // 2, pl.ds(part * rows, rows), lanes_of(local, comp)] = block[local * rows : (local + 1) * rows]
            return carry

        lax.fori_loop(0, count, arrive, 0)

        def compute(pair, carry):
            field = mm(forward_ref[...], stacked_values(store[pair]))
            values = field[:planes]
            along_z = field[planes:]
            results = []
            for which in range(2):
                vel = [values[:, lanes_of(which, comp)] for comp in range(comps)]
                part = geo[pair * 2 + which]
                along_first = vel[0] * part[0:1] + vel[1] * part[2:3]
                along_second = vel[0] * part[1:2] + vel[1] * part[3:4]
                for comp in range(comps):
                    high, low = split(vel[comp])
                    slopes = mm(jnp.concatenate([high, low], axis=1), deriv_ref[: 2 * LANES]) + mm(high, deriv_ref[2 * LANES :])
                    results.append(
                        slopes[:, :LANES] * along_first
                        + slopes[:, LANES:] * along_second
                        + vel[2] * along_z[:, lanes_of(which, comp)]
                    )
            store[pair] = mm(backward_ref[...], stacked_values(jnp.concatenate(results, axis=1)))
            return carry

        lax.fori_loop(0, pairs, compute, 0)

        def leave(part, carry):
            for comp in range(comps):
                block = jnp.concatenate(
                    [store[local // 2, pl.ds(part * rows, rows), lanes_of(local, comp)] for local in range(per)], axis=0
                )
                dst[part, comp] = block.T[:points]
            return carry

        lax.fori_loop(0, count, leave, 0)

    return pl.pallas_call(
        kernel,
        out_shape=jax.ShapeDtypeStruct(received.shape, F32),
        scratch_shapes=[pltpu.VMEM((pairs, planes, width), F32)],
        compiler_params=params(),
        name="advect",
    )(received, geometry, forward, backward, deriv)


def lift_parts(sent, returned, lift_rows, kind_lanes, side):
    count, comps, points, _ = sent.shape
    wide = count * LANES
    half = wide // 2

    def kernel(vel, hat, weights, kinds, side_ref, mid, own, away):
        for part in range(count):
            mid[part, 0] = vel[part, 0] - STEP_DT * hat[part, 0]
        field = jnp.concatenate([mid[part, 0] for part in range(count)], axis=1)
        high, low = split(SIGMA_COEF * field)
        w_high, w_low = split(weights[...])
        both = mm(w_high, high) + (mm(w_high, low) + mm(w_low, high))
        lifted = jnp.where(kinds[0:1] > 0.5, both[4 * SUB :], both[: 4 * SUB])
        bit = lax.broadcasted_iota(jnp.int32, (4 * SUB, LANES), 1) // 8 % 2 == 0
        second = side_ref[0:1] > 0.5
        for tile in range(count // 2):
            even = lifted[:, 2 * tile * LANES : (2 * tile + 1) * LANES]
            odd = lifted[:, (2 * tile + 1) * LANES : (2 * tile + 2) * LANES]
            low_rows = jnp.where(bit, even, pltpu.roll(odd, 8, 1))
            high_rows = jnp.where(bit, pltpu.roll(even, LANES - 8, 1), odd)
            at = slice(tile * LANES, (tile + 1) * LANES)
            own[0, :, at] = jnp.where(second, high_rows, low_rows)
            away[0, :, at] = jnp.where(second, low_rows, high_rows)

    block = pl.BlockSpec((count, 1, points, LANES), lambda c: (0, c, 0, 0))
    piece = pl.BlockSpec((1, 4 * SUB, half), lambda c: (c, 0, 0))
    return pl.pallas_call(
        kernel,
        grid=(comps,),
        in_specs=[block, block, whole_spec(lift_rows.shape), whole_spec(kind_lanes.shape), whole_spec(side.shape)],
        out_specs=[block, piece, piece],
        out_shape=[
            jax.ShapeDtypeStruct(sent.shape, F32),
            jax.ShapeDtypeStruct((comps, 4 * SUB, half), F32),
            jax.ShapeDtypeStruct((comps, 4 * SUB, half), F32),
        ],
        compiler_params=params(),
        name="lift_parts",
    )(sent, returned, lift_rows, kind_lanes, side)


def solve_traces(own, other, own_facts, other_facts, lam_lanes, side, matrices):
    comps, _, half = own.shape
    wide = 2 * half
    column = COLUMN_ELEMS // SUB * LANES

    def kernel(own_ref, other_ref, own_fact, other_fact, lam_ref, side_ref, weights, mine, away):
        second = jnp.concatenate([side_ref[0:1]] * (half // LANES), axis=1) > 0.5

        def joined(first, last):
            return jnp.concatenate([jnp.where(second, last, first), jnp.where(second, first, last)], axis=1)

        facts = joined(own_fact[...], other_fact[...])
        free_v = facts[:SUB]
        free_h = facts[SUB : 2 * SUB]
        is_second = facts[2 * SUB : 2 * SUB + 1] > 0.5
        scale = facts[2 * SUB + 1 : 2 * SUB + 2]
        lam = lam_ref[0:1]
        w_all = stacked_weights(weights[...])
        lane = lax.broadcasted_iota(jnp.int32, (1, wide), 1)
        along = lane % LANES // SUB
        odd_half = lane // 8 % 2 == 1
        tile = lane // LANES
        per_column = COLUMN_ELEMS // SUB
        top_edge = (tile % per_column == per_column - 1) & odd_half & (along == SUB // 2 - 1)
        low_edge = (tile % per_column == 0) & jnp.logical_not(odd_half) & (along == 0)

        def above(x):
            last = jnp.where(odd_half, pltpu.roll(x, wide - 8, 1), pltpu.roll(x, 104, 1))
            moved = jnp.where(along < SUB // 2 - 1, pltpu.roll(x, wide - 16, 1), last)
            return jnp.where(top_edge, 0.0, moved)

        def below(x):
            head = jnp.where(odd_half, pltpu.roll(x, wide - 104, 1), pltpu.roll(x, 8, 1))
            moved = jnp.where(along > 0, pltpu.roll(x, 16, 1), head)
            return jnp.where(low_edge, 0.0, moved)

        edge = jnp.zeros((SUB, column), F32)

        def vector_of(v, h):
            right = jnp.concatenate([v[:, column:], edge], axis=1)
            return jnp.concatenate([v, right, h, above(h)], axis=0)

        def gather(parts):
            right = jnp.concatenate([edge, parts[SUB : 2 * SUB, :-column]], axis=1)
            v = (parts[:SUB] + right) * free_v
            h = (parts[2 * SUB : 3 * SUB] + below(parts[3 * SUB :])) * free_h
            return v, h

        def total(product):
            acc = product[:, :LANES]
            for at in range(1, wide // LANES):
                acc = acc + product[:, at * LANES : (at + 1) * LANES]
            acc = jnp.sum(acc, axis=0, keepdims=True)
            acc = jnp.broadcast_to(acc, (8, LANES))
            for step in (8, 16, 32, 64):
                acc = acc + pltpu.roll(acc, step, 1)
            return acc[0:1]

        def spread(row):
            return jnp.concatenate([row] * (wide // LANES), axis=1)

        res_v, res_h = gather(joined(own_ref[0], other_ref[0]))
        now = total(res_v * res_v + res_h * res_h)
        zero = jnp.zeros_like(res_v)

        def sweep(_, state):
            tr_v, tr_h, res_v, res_h, dir_v, dir_h, now = state
            both = mm(w_all, stacked_values(vector_of(dir_v, dir_h)))
            rows = 4 * SUB
            stiff = jnp.where(is_second, both[rows : 2 * rows], both[:rows])
            mass = jnp.where(is_second, both[3 * rows :], both[2 * rows : 3 * rows])
            im_v, im_h = gather(scale * (stiff + lam * mass))
            alpha = spread(now / total(dir_v * im_v + dir_h * im_h))
            tr_v, tr_h = tr_v + alpha * dir_v, tr_h + alpha * dir_h
            res_v, res_h = res_v - alpha * im_v, res_h - alpha * im_h
            fresh = total(res_v * res_v + res_h * res_h)
            ratio = spread(fresh / now)
            return tr_v, tr_h, res_v, res_h, res_v + ratio * dir_v, res_h + ratio * dir_h, fresh

        state = lax.fori_loop(0, CG_STEPS, sweep, (zero, zero, res_v, res_h, res_v, res_h, now))
        vector = vector_of(state[0], state[1])
        mine[0] = jnp.where(second, vector[:, half:], vector[:, :half])
        away[0] = jnp.where(second, vector[:, :half], vector[:, half:])

    piece = pl.BlockSpec((1, 4 * SUB, half), lambda c: (c, 0, 0))
    shape = jax.ShapeDtypeStruct(own.shape, F32)
    extra = (own_facts, other_facts, lam_lanes, side, matrices)
    return pl.pallas_call(
        kernel,
        grid=(comps,),
        in_specs=[piece, piece] + [whole_spec(item.shape) for item in extra],
        out_specs=[piece, piece],
        out_shape=[shape, shape],
        compiler_params=params(),
        name="solve_traces",
    )(own, other, *extra)


def recover_nodes(mid, mine, other, side, kind_lanes, weight_lanes, recover_cols, rows):
    count, comps, points, _ = mid.shape
    half = mine.shape[2]
    per = LANES // rows
    nodes = count * per * points
    second_at = recover_cols.shape[0] // 2

    def kernel(mid_ref, mine_ref, other_ref, side_ref, kinds, factor, weights, out):
        second = side_ref[0:1] > 0.5
        bit = lax.broadcasted_iota(jnp.int32, (4 * SUB, LANES), 1) // 8 % 2 == 0
        tiles = []
        for tile in range(half // LANES):
            at = slice(tile * LANES, (tile + 1) * LANES)
            first_half = mine_ref[0, :, at]
            last_half = other_ref[0, :, at]
            low_rows = jnp.where(second, last_half, first_half)
            high_rows = jnp.where(second, first_half, last_half)
            tiles.append(jnp.where(bit, low_rows, pltpu.roll(high_rows, 8, 1)))
            tiles.append(jnp.where(bit, pltpu.roll(low_rows, LANES - 8, 1), high_rows))
        both = mm(stacked_weights(weights[...]), stacked_values(jnp.concatenate(tiles, axis=1)))
        found = jnp.where(kinds[0:1] > 0.5, both[second_at : second_at + points], both[:points])
        for part in range(count):
            at = slice(part * LANES, (part + 1) * LANES)
            block = mid_ref[part, 0] * factor[0:1, at] + found[:, at]
            block = jnp.concatenate([block, jnp.zeros((LANES - points, LANES), F32)], axis=0).T
            for local in range(per):
                start = (part * per + local) * points
                out[0, :, start : start + points] = block[local * rows : (local + 1) * rows, :points]

    piece = pl.BlockSpec((1, 4 * SUB, half), lambda c: (c, 0, 0))
    extra = (side, kind_lanes, weight_lanes, recover_cols)
    return pl.pallas_call(
        kernel,
        grid=(comps,),
        in_specs=[pl.BlockSpec((count, 1, points, LANES), lambda c: (0, c, 0, 0)), piece, piece]
        + [whole_spec(item.shape) for item in extra],
        out_specs=pl.BlockSpec((1, rows, nodes), lambda c: (c, 0, 0)),
        out_shape=jax.ShapeDtypeStruct((comps, rows, nodes), F32),
        compiler_params=params(),
        name="recover_nodes",
    )(mid, mine, other, *extra)


def edge_rows(matrix):
    shape = matrix.shape
    grouped = matrix.reshape(shape[0], 4, QUAD, shape[2])
    grouped = jnp.pad(grouped, ((0, 0), (0, 0), (0, SUB - QUAD), (0, 0)))
    return grouped.reshape(shape[0], 4 * SUB, shape[2])


def edge_cols(matrix):
    return edge_rows(matrix.swapaxes(1, 2)).swapaxes(1, 2)


def fast_device(
    velocity,
    geometry,
    element_kind,
    element_scale,
    dirichlet,
    schur_stiffness,
    schur_mass,
    lift,
    recover,
):
    count = lax.axis_size("planes")
    rows = velocity.shape[1]
    elems = element_kind.shape[0]
    points = QUAD * QUAD
    per = elems // count
    core = lax.axis_index("elem")
    place = lax.axis_index("planes")
    side = jnp.broadcast_to(core.astype(F32), (8, LANES))

    free = jnp.pad((1 - dirichlet).astype(F32), ((0, 0), (0, SUB - QUAD), (0, 0))).reshape(2 * SUB, elems)
    facts = jnp.concatenate(
        [free, (element_kind == 1).astype(F32)[None], element_scale[None], jnp.zeros((6, elems), F32)], axis=0
    )
    facts = facts.reshape(facts.shape[0], elems // 16, 2, 8).swapaxes(2, 3)
    facts = jnp.broadcast_to(facts[..., None], facts.shape + (8,)).reshape(facts.shape[0], elems * 8)
    swap = [(0, 1), (1, 0)]
    other_facts = lax.ppermute(facts, "elem", swap)

    def lam_of(row):
        return SIGMA_COEF + (BETA_COEF * ((row + 1) // 2).astype(F32)) ** 2

    lane = jnp.arange(count * LANES, dtype=jnp.int32)
    lam_half = lam_of(place * rows + core * 8 + lane % 8)
    lam_lanes = jnp.broadcast_to(lam_half[None], (8, lane.shape[0]))
    weight = SIGMA_COEF / (SIGMA_COEF + lam_of(place * rows + lane % rows))
    weight_lanes = jnp.broadcast_to(weight[None], (8, lane.shape[0]))
    kinds = jnp.broadcast_to((element_kind == 1).astype(F32)[None, :, None], (8, elems, rows)).reshape(8, elems * rows)
    geo = lax.dynamic_slice_in_dim(geometry.reshape(4, elems, points), place * per, per, 1)
    geo = jnp.pad(geo.swapaxes(0, 1), ((0, 0), (0, 4), (0, LANES - points)))

    sent = pack_messages(velocity, count)
    received = lax.all_to_all(sent, "planes", split_axis=0, concat_axis=0, tiled=True)
    hats = advect(received, geo, count * rows, rows)
    returned = lax.all_to_all(hats, "planes", split_axis=0, concat_axis=0, tiled=True)

    lift_rows = edge_rows(lift).reshape(8 * SUB, points)
    mid, own, away = lift_parts(sent, returned, lift_rows, kinds, side)
    other = lax.ppermute(away, "elem", swap)
    matrices = jnp.concatenate([schur_stiffness, schur_mass], axis=0)
    matrices = edge_cols(edge_rows(matrices)).reshape(16 * SUB, 4 * SUB)
    mine, away = solve_traces(own, other, facts, other_facts, lam_lanes, side, matrices)
    other = lax.ppermute(away, "elem", swap)
    recover_cols = jnp.pad(edge_cols(recover), ((0, 0), (0, 88 - points), (0, 0))).reshape(2 * 88, 4 * SUB)
    return recover_nodes(mid, mine, other, side, kinds, weight_lanes, recover_cols, rows)


def per_device(velocity, geometry, element_kind, *rest):
    count = lax.axis_size("planes")
    rows = velocity.shape[1]
    elems = element_kind.shape[0]
    fits = rows == 16 and elems == LANES and elems * rows == count * LANES and lax.axis_size("elem") == 2
    body = fast_device if fits else plain_device
    return body(velocity, geometry, element_kind, *rest)


def solution(mesh):
    in_specs = (
        P(None, "planes", "elem"),
        P(None, "elem"),
        P("elem"),
        P("elem"),
        P(None, None, "elem"),
        P(),
        P(),
        P(),
        P(),
    )
    out_specs = P(None, "planes", "elem")
    return jax.shard_map(
        per_device, mesh=mesh, in_specs=in_specs, out_specs=out_specs, check_vma=False
    )
```

```python
import math

import jax
import jax.numpy as jnp
import numpy as np
from jax import lax
from jax.experimental import pallas as pl
from jax.experimental.pallas import tpu as pltpu
from jax.sharding import PartitionSpec as P

PLANES = 256
QUAD = 9
COLUMN_ELEMS = 32
CG_STEPS = 4


HIGHEST = lax.Precision.HIGHEST
SIGMA_COEF = 1.0
BETA_COEF = 0.01
STEP_DT = 0.002


def passed_along(value, axis, steps):
    count = lax.axis_size(axis)
    leading, last = (max(0, -steps), min(count, count - steps))
    return lax.ppermute(value, axis, [(source, source + steps) for source in range(leading, last)])


def gauss_derivative(points):
    nodes = -np.cos(np.pi * (2 * np.arange(points) + 1) / (2 * points))
    ident = np.eye(points)
    diffs = nodes[:, None] - nodes[None, :] + ident
    weights = 1.0 / np.prod(diffs, axis=1)
    matrix = weights[None, :] / weights[:, None] / diffs
    matrix = matrix * (1.0 - ident)
    return matrix - ident * matrix.sum(axis=1)[:, None]


def kron_tables():
    deriv = gauss_derivative(QUAD)
    identity = np.eye(QUAD)
    return (
        jnp.asarray(np.kron(deriv, identity), jnp.float32),
        jnp.asarray(np.kron(identity, deriv), jnp.float32),
    )


def fourier_tables(planes):
    zeta = jnp.arange(planes, dtype=jnp.int32)
    rows = jnp.arange(planes, dtype=jnp.int32)
    waves = (rows + 1) // 2
    phase = waves[None, :] * zeta[:, None] % planes
    angle = 2.0 * math.pi / planes * phase.astype(jnp.float32)
    cosine = jnp.cos(angle)
    sine = jnp.sin(angle)
    odd = (rows % 2 == 1)[None, :]
    first = (rows == 0)[None, :]
    last = (rows == planes - 1)[None, :]
    synth = jnp.where(first, 1.0, jnp.where(odd, cosine, sine))
    rate = BETA_COEF * waves.astype(jnp.float32)[None, :]
    slope = jnp.where(first | last, 0.0, jnp.where(odd, -rate * sine, rate * cosine))
    weight = jnp.where((rows == 0) | (rows == planes - 1), 1.0 / planes, 2.0 / planes).astype(
        jnp.float32
    )
    analysis = synth.T * weight[:, None]
    return (synth, slope, analysis)


def inner(first_pair, second_pair):
    return jnp.sum(first_pair[0] * second_pair[0], axis=(0, 2)) + jnp.sum(
        first_pair[1] * second_pair[1], axis=(0, 2)
    )


def global_total(first_pair, second_pair):
    return lax.psum(inner(first_pair, second_pair), "elem")


def global_squares(pair):
    return lax.psum(inner(pair, pair), "elem")


def assemble(outputs, incoming, free):
    left = outputs[:QUAD]
    right = outputs[QUAD : 2 * QUAD]
    bottom = outputs[2 * QUAD : 3 * QUAD]
    top = outputs[3 * QUAD :]
    vertical = left + jnp.concatenate([incoming, right[:, :, :-COLUMN_ELEMS]], axis=2)
    grid = top.reshape(top.shape[0], top.shape[1], -1, COLUMN_ELEMS)
    shifted = jnp.concatenate([jnp.zeros_like(grid[..., :1]), grid[..., :-1]], axis=3).reshape(
        bottom.shape
    )
    horizontal = bottom + shifted
    return (vertical * free[0], horizontal * free[1])


def plain_device(
    velocity,
    geometry,
    element_kind,
    element_scale,
    dirichlet,
    schur_stiffness,
    schur_mass,
    lift,
    recover,
):
    first, second = kron_tables()
    synth, slope, analysis = fourier_tables(PLANES)
    local_rows = velocity.shape[1]
    node_count = velocity.shape[2]
    share = node_count // lax.axis_size("planes")
    geo_part = lax.dynamic_slice_in_dim(geometry, lax.axis_index("planes") * share, share, 1)

    def transform(table, field):
        return jnp.einsum("zr,crm->czm", table, field, precision=HIGHEST)

    items = lax.all_to_all(velocity, "planes", split_axis=2, concat_axis=1, tiled=True)
    values = transform(synth, items)
    along_z = transform(slope, items)
    shaped = values.reshape(values.shape[:-1] + (-1, QUAD * QUAD))
    along_r = jnp.einsum("...en,mn->...em", shaped, first, precision=HIGHEST).reshape(values.shape)
    along_s = jnp.einsum("...en,mn->...em", shaped, second, precision=HIGHEST).reshape(values.shape)
    along_x = geo_part[0] * along_r + geo_part[1] * along_s
    along_y = geo_part[2] * along_r + geo_part[3] * along_s
    values, along_x, along_y, along_z = (values, along_x, along_y, along_z)
    advection = values[0] * along_x + values[1] * along_y + values[2] * along_z
    advection_hat = jnp.einsum("rz,czm->crm", analysis, advection, precision=HIGHEST)
    returned = lax.all_to_all(advection_hat, "planes", split_axis=1, concat_axis=2, tiled=True)
    intermediate = velocity - STEP_DT * returned
    elem_count = element_kind.shape[0]
    row_count = 3 * local_rows
    waves = (
        (lax.axis_index("planes") * local_rows + jnp.arange(local_rows, dtype=jnp.int32) + 1) // 2
    ).astype(jnp.float32)
    lam = jnp.tile(SIGMA_COEF + (BETA_COEF * waves) ** 2, 3)
    free = (1 - dirichlet).astype(jnp.float32)[:, :, None, :]
    chooser = (element_kind == 1).astype(jnp.float32)

    def element_apply(vector, kinds, scales):
        flat = vector.reshape(vector.shape[0], -1)
        results = []
        for kind in range(2):
            stiff = jnp.dot(schur_stiffness[kind], flat, precision=HIGHEST).reshape(vector.shape)
            massed = jnp.dot(schur_mass[kind], flat, precision=HIGHEST).reshape(vector.shape)
            results.append(stiff + lam[None, :, None] * massed)
        return scales[None, None, :] * jnp.where(kinds[None, None, :] > 0.5, results[1], results[0])

    def element_vector(vertical, horizontal):
        arriving = passed_along(vertical[:, :, :COLUMN_ELEMS], "elem", -1)
        right = jnp.concatenate([vertical[:, :, COLUMN_ELEMS:], arriving], axis=2)
        grid = horizontal.reshape(horizontal.shape[0], horizontal.shape[1], -1, COLUMN_ELEMS)
        top = jnp.concatenate([grid[..., 1:], jnp.zeros_like(grid[..., :1])], axis=3).reshape(
            horizontal.shape
        )
        return jnp.concatenate([vertical, right, horizontal, top], axis=0)

    node_values = (SIGMA_COEF * intermediate).reshape(row_count, elem_count, QUAD * QUAD)
    lifted = jnp.where(
        chooser[None, None, :] > 0.5,
        jnp.einsum("kn,ren->kre", lift[1], node_values, precision=HIGHEST),
        jnp.einsum("kn,ren->kre", lift[0], node_values, precision=HIGHEST),
    )
    lifted_right = passed_along(lifted[QUAD : 2 * QUAD, :, -COLUMN_ELEMS:], "elem", 1)
    forcing = assemble(lifted, lifted_right, free)
    trace = (jnp.zeros_like(forcing[0]), jnp.zeros_like(forcing[1]))
    residual = forcing
    direction = forcing
    norm_now = global_squares(residual)
    for sweep in range(CG_STEPS):
        outputs = element_apply(element_vector(direction[0], direction[1]), chooser, element_scale)
        operator_arriving = passed_along(outputs[QUAD : 2 * QUAD, :, -COLUMN_ELEMS:], "elem", 1)
        image = assemble(outputs, operator_arriving, free)
        alpha = (norm_now / global_total(direction, image))[None, :, None]
        trace = (trace[0] + alpha * direction[0], trace[1] + alpha * direction[1])
        residual = (residual[0] - alpha * image[0], residual[1] - alpha * image[1])
        norm_next = global_squares(residual)
        ratio = (norm_next / norm_now)[None, :, None]
        direction = (residual[0] + ratio * direction[0], residual[1] + ratio * direction[1])
        norm_now = norm_next
    vector = element_vector(trace[0], trace[1])
    recovered = jnp.where(
        chooser[None, :, None] > 0.5,
        jnp.einsum("nl,lre->ren", recover[1], vector, precision=HIGHEST),
        jnp.einsum("nl,lre->ren", recover[0], vector, precision=HIGHEST),
    )
    weight = SIGMA_COEF / (SIGMA_COEF + lam)
    result = (
        intermediate.reshape(row_count, elem_count, QUAD * QUAD) * weight[:, None, None] + recovered
    )
    return result.reshape(velocity.shape)


LANES = 128
SUB = 16
F32 = jnp.float32
BF16 = jnp.bfloat16


def split(value):
    high = value.astype(BF16)
    return high, (value - high.astype(F32)).astype(BF16)


def np_split(value):
    high = np.asarray(value, np.float32).astype(BF16)
    low = (np.asarray(value, np.float64) - high.astype(np.float64)).astype(np.float32).astype(BF16)
    return high, low


def mm(first, second):
    return jnp.dot(first, second, preferred_element_type=F32)


def stacked_weights(weights):
    high, low = split(weights)
    return jnp.concatenate([high, high, low], axis=1)


def stacked_values(values):
    high, low = split(values)
    return jnp.concatenate([high, low, high], axis=0)


def advect_tables(planes):
    zeta = np.arange(planes)
    rows = np.arange(planes)
    waves = (rows + 1) // 2
    angle = 2.0 * np.pi / planes * ((waves[None, :] * zeta[:, None]) % planes)
    odd = (rows % 2 == 1)[None, :]
    first = (rows == 0)[None, :]
    last = (rows == planes - 1)[None, :]
    synth = np.where(first, 1.0, np.where(odd, np.cos(angle), np.sin(angle)))
    rate = BETA_COEF * waves[None, :]
    slope = np.where(first | last, 0.0, np.where(odd, -rate * np.sin(angle), rate * np.cos(angle)))
    weight = np.where((rows == 0) | (rows == planes - 1), 1.0 / planes, 2.0 / planes)
    analysis = synth.T * weight[:, None]
    high, low = np_split(np.concatenate([synth, slope], axis=0))
    forward = np.concatenate([high, high, low], axis=1)
    high, low = np_split(analysis)
    backward = np.concatenate([high, high, low], axis=1)
    points = QUAD * QUAD
    deriv = gauss_derivative(QUAD)
    both = np.zeros((LANES, 2 * LANES))
    both[:points, :points] = np.kron(deriv, np.eye(QUAD)).T
    both[:points, LANES : LANES + points] = np.kron(np.eye(QUAD), deriv).T
    high, low = np_split(both)
    return jnp.asarray(forward), jnp.asarray(backward), jnp.asarray(np.concatenate([high, high, low], axis=0))


def whole_spec(shape):
    return pl.BlockSpec(shape, lambda *_: (0,) * len(shape))


def params():
    return pltpu.CompilerParams(vmem_limit_bytes=60 * 1024 * 1024)


def solve_rows(own, other, own_fact, other_fact, lam, side_row, weights):
    half = own.shape[1]
    wide = 2 * half
    column = COLUMN_ELEMS // SUB * LANES
    second = jnp.concatenate([side_row] * (half // LANES), axis=1) > 0.5

    def joined(first, last):
        return jnp.concatenate([jnp.where(second, last, first), jnp.where(second, first, last)], axis=1)

    facts = joined(own_fact, other_fact)
    free_v = facts[:SUB]
    free_h = facts[SUB : 2 * SUB]
    is_second = facts[2 * SUB : 2 * SUB + 1] > 0.5
    scale = facts[2 * SUB + 1 : 2 * SUB + 2]
    w_all = stacked_weights(weights)
    lane = lax.broadcasted_iota(jnp.int32, (1, wide), 1)
    along = lane % LANES // SUB
    odd_half = lane // 8 % 2 == 1
    tile = lane // LANES
    per_column = COLUMN_ELEMS // SUB
    top_edge = (tile % per_column == per_column - 1) & odd_half & (along == SUB // 2 - 1)
    low_edge = (tile % per_column == 0) & jnp.logical_not(odd_half) & (along == 0)

    def above(x):
        last = jnp.where(odd_half, pltpu.roll(x, wide - 8, 1), pltpu.roll(x, 104, 1))
        moved = jnp.where(along < SUB // 2 - 1, pltpu.roll(x, wide - 16, 1), last)
        return jnp.where(top_edge, 0.0, moved)

    def below(x):
        head = jnp.where(odd_half, pltpu.roll(x, wide - 104, 1), pltpu.roll(x, 8, 1))
        moved = jnp.where(along > 0, pltpu.roll(x, 16, 1), head)
        return jnp.where(low_edge, 0.0, moved)

    edge = jnp.zeros((SUB, column), F32)

    def vector_of(v, h):
        right = jnp.concatenate([v[:, column:], edge], axis=1)
        return jnp.concatenate([v, right, h, above(h)], axis=0)

    def gather(parts):
        right = jnp.concatenate([edge, parts[SUB : 2 * SUB, :-column]], axis=1)
        v = (parts[:SUB] + right) * free_v
        h = (parts[2 * SUB : 3 * SUB] + below(parts[3 * SUB :])) * free_h
        return v, h

    def total(product):
        acc = product[:, :LANES]
        for at in range(1, wide // LANES):
            acc = acc + product[:, at * LANES : (at + 1) * LANES]
        acc = jnp.sum(acc, axis=0, keepdims=True)
        acc = jnp.broadcast_to(acc, (8, LANES))
        for step in (8, 16, 32, 64):
            acc = acc + pltpu.roll(acc, step, 1)
        return acc[0:1]

    def spread(row):
        return jnp.concatenate([row] * (wide // LANES), axis=1)

    res_v, res_h = gather(joined(own, other))
    now = total(res_v * res_v + res_h * res_h)
    zero = jnp.zeros_like(res_v)

    def sweep(_, state):
        tr_v, tr_h, res_v, res_h, dir_v, dir_h, now = state
        both = mm(w_all, stacked_values(vector_of(dir_v, dir_h)))
        rows = 4 * SUB
        stiff = jnp.where(is_second, both[rows : 2 * rows], both[:rows])
        mass = jnp.where(is_second, both[3 * rows :], both[2 * rows : 3 * rows])
        im_v, im_h = gather(scale * (stiff + lam * mass))
        alpha = spread(now / total(dir_v * im_v + dir_h * im_h))
        tr_v, tr_h = tr_v + alpha * dir_v, tr_h + alpha * dir_h
        res_v, res_h = res_v - alpha * im_v, res_h - alpha * im_h
        fresh = total(res_v * res_v + res_h * res_h)
        ratio = spread(fresh / now)
        return tr_v, tr_h, res_v, res_h, res_v + ratio * dir_v, res_h + ratio * dir_h, fresh

    state = lax.fori_loop(0, CG_STEPS, sweep, (zero, zero, res_v, res_h, res_v, res_h, now))
    vector = vector_of(state[0], state[1])
    mine = jnp.where(second, vector[:, half:], vector[:, :half])
    away = jnp.where(second, vector[:, :half], vector[:, half:])
    return mine, away


def advect_and_solve(velocity, geometry, lift_rows, kind_lanes, side, facts, lam_lanes, matrices, count):
    comps, rows, nodes = velocity.shape
    points = QUAD * QUAD
    per = LANES // rows
    pairs = per // 2
    planes = count * rows
    half = count * LANES // 2
    forward, backward, deriv = advect_tables(planes)

    def kernel(
        vel_ref, geo, forward_ref, backward_ref, deriv_ref, lift_ref, kinds, side_ref, facts_ref, lam_ref, mat_ref,
        mid, mine_out, other_out,
        sent, recv, hats, ret, store, fields, slopes, own, away, other, traces, their_traces, facts_out, their_facts,
        send_sem, recv_sem, pair_send, pair_recv,
    ):
        me = lax.axis_index("planes")
        core = lax.axis_index("elem")
        barrier = pltpu.get_barrier_semaphore()

        def greet(step, carry):
            pl.semaphore_signal(
                barrier, inc=1, device_id={"planes": lax.rem(me + step, count)}, device_id_type=pl.DeviceIdType.MESH
            )
            return carry

        lax.fori_loop(1, count, greet, 0)
        pl.semaphore_signal(barrier, inc=1, device_id={"elem": 1 - core}, device_id_type=pl.DeviceIdType.MESH)

        def copy_to(source, target, way, comp, peer):
            return pltpu.make_async_remote_copy(
                src_ref=source.at[comp, peer],
                dst_ref=target.at[comp, me],
                send_sem=send_sem.at[way, comp, peer],
                recv_sem=recv_sem.at[way, comp, me],
                device_id={"planes": peer},
                device_id_type=pl.DeviceIdType.MESH,
            )

        def copy_from(source, target, way, comp, peer):
            return pltpu.make_async_remote_copy(
                src_ref=source.at[comp, peer],
                dst_ref=target.at[comp, peer],
                send_sem=send_sem.at[way, comp, peer],
                recv_sem=recv_sem.at[way, comp, peer],
                device_id={"planes": peer},
                device_id_type=pl.DeviceIdType.MESH,
            )

        def start_all(source, target, way, comp):
            def one(step, carry):
                copy_to(source, target, way, comp, lax.rem(me + count // 2 + step, count)).start()
                return carry

            lax.fori_loop(0, count // 2, one, 0)

            def two(step, carry):
                copy_to(source, target, way, comp, lax.rem(me + step, count)).start()
                return carry

            lax.fori_loop(1, count // 2, two, 0)

        def pair_copy(source, target, at):
            return pltpu.make_async_remote_copy(
                src_ref=source,
                dst_ref=target,
                send_sem=pair_send.at[at],
                recv_sem=pair_recv.at[at],
                device_id={"elem": 1 - core},
                device_id_type=pl.DeviceIdType.MESH,
            )

        def pack(comp):
            for part in range(count):
                pieces = []
                for local in range(per):
                    at = (part * per + local) * points
                    pieces.append(vel_ref[comp, :, at : at + points])
                sent[comp, part] = jnp.concatenate(pieces, axis=0).T

        def arrive(comp, part, block):
            block = jnp.concatenate([block, jnp.zeros((LANES - points, LANES), F32)], axis=0).T
            for local in range(per):
                at = local % 2 * LANES
                store[local // 2, pl.ds(pl.multiple_of(part * rows, rows), rows), at : at + LANES] = block[
                    local * rows : (local + 1) * rows
                ]

        def arrive_all(comp):
            arrive(comp, me, sent[comp, me])

            def one(step, carry):
                part = lax.rem(me + step, count)
                copy_from(sent, recv, 0, comp, part).wait_recv()
                arrive(comp, part, recv[comp, part])
                return carry

            lax.fori_loop(count // 2, count, one, 0)
            lax.fori_loop(1, count // 2, one, 0)

        def synthesize(comp):
            def one(pair, carry):
                field = mm(forward_ref[...], stacked_values(store[pair]))
                fields[comp, pair] = field
                for which in range(2):
                    high, low = split(field[:planes, which * LANES : (which + 1) * LANES])
                    slopes[comp, pair, which] = mm(jnp.concatenate([high, low], axis=1), deriv_ref[: 2 * LANES]) + mm(
                        high, deriv_ref[2 * LANES :]
                    )
                return carry

            lax.fori_loop(0, pairs, one, 0)

        def advect(comp):
            def one(pair, carry):
                results = []
                for which in range(2):
                    at = slice(which * LANES, (which + 1) * LANES)
                    vel = [fields[item, pair, :planes, at] for item in range(comps)]
                    part = geo[pair * 2 + which]
                    results.append(
                        slopes[comp, pair, which, :, :LANES] * (vel[0] * part[0:1] + vel[1] * part[2:3])
                        + slopes[comp, pair, which, :, LANES:] * (vel[0] * part[1:2] + vel[1] * part[3:4])
                        + vel[2] * fields[comp, pair, planes:, at]
                    )
                store[pair] = mm(backward_ref[...], stacked_values(jnp.concatenate(results, axis=1)))
                return carry

            lax.fori_loop(0, pairs, one, 0)
            for part in range(count):
                block = jnp.concatenate(
                    [
                        store[local // 2, part * rows : (part + 1) * rows, local % 2 * LANES : (local % 2 + 1) * LANES]
                        for local in range(per)
                    ],
                    axis=0,
                )
                hats[comp, part] = block.T[:points]

        def lift(comp):
            def one(step, carry):
                copy_from(hats, ret, 1, comp, lax.rem(me + step, count)).wait_recv()
                return carry

            lax.fori_loop(1, count, one, 0)
            ret[comp, me] = hats[comp, me]
            for part in range(count):
                mid[comp, part] = sent[comp, part] - STEP_DT * ret[comp, part]
            field = jnp.concatenate([mid[comp, part] for part in range(count)], axis=1)
            high, low = split(SIGMA_COEF * field)
            w_high, w_low = split(lift_ref[...])
            both = mm(w_high, high) + (mm(w_high, low) + mm(w_low, high))
            lifted = jnp.where(kinds[0:1] > 0.5, both[4 * SUB :], both[: 4 * SUB])
            bit = lax.broadcasted_iota(jnp.int32, (4 * SUB, LANES), 1) // 8 % 2 == 0
            second = side_ref[0:1] > 0.5
            for tile in range(count // 2):
                even = lifted[:, 2 * tile * LANES : (2 * tile + 1) * LANES]
                odd = lifted[:, (2 * tile + 1) * LANES : (2 * tile + 2) * LANES]
                low_rows = jnp.where(bit, even, pltpu.roll(odd, 8, 1))
                high_rows = jnp.where(bit, pltpu.roll(even, LANES - 8, 1), odd)
                at = slice(tile * LANES, (tile + 1) * LANES)
                own[comp, :, at] = jnp.where(second, high_rows, low_rows)
                away[comp, :, at] = jnp.where(second, low_rows, high_rows)
            pair_copy(away.at[comp], other.at[comp], comp).start()

        def solve(comp):
            pair_copy(away.at[comp], other.at[comp], comp).wait_recv()
            mine, theirs = solve_rows(
                own[comp], other[comp], facts_ref[...], their_facts[...], lam_ref[0:1], side_ref[0:1], mat_ref[...]
            )
            mine_out[comp] = mine
            traces[comp] = theirs
            pair_copy(traces.at[comp], their_traces.at[comp], comps + comp).start()

        facts_out[...] = facts_ref[...]
        pack(0)
        pl.semaphore_wait(barrier, count)
        start_all(sent, recv, 0, 0)
        pair_copy(facts_out, their_facts, 2 * comps).start()
        for comp in range(1, comps):
            pack(comp)
            start_all(sent, recv, 0, comp)
        for comp in range(comps):
            arrive_all(comp)
            synthesize(comp)
        for comp in range(comps):
            advect(comp)
            start_all(hats, ret, 1, comp)
        pair_copy(facts_out, their_facts, 2 * comps).wait_recv()
        for comp in range(comps):
            lift(comp)
            solve(comp)
        for comp in range(comps):
            pair_copy(traces.at[comp], their_traces.at[comp], comps + comp).wait_recv()
            other_out[comp] = their_traces[comp]
        pair_copy(facts_out, their_facts, 2 * comps).wait_send()
        for comp in range(comps):
            pair_copy(away.at[comp], other.at[comp], comp).wait_send()
            pair_copy(traces.at[comp], their_traces.at[comp], comps + comp).wait_send()

            def drain(step, carry):
                peer = lax.rem(me + step, count)
                copy_to(sent, recv, 0, comp, peer).wait_send()
                copy_to(hats, ret, 1, comp, peer).wait_send()
                return carry

            lax.fori_loop(1, count, drain, 0)

    message = (comps, count, points, LANES)
    piece = (comps, 4 * SUB, half)
    operands = (velocity, geometry, forward, backward, deriv, lift_rows, kind_lanes, side, facts, lam_lanes, matrices)
    vmem = pl.BlockSpec(memory_space=pltpu.VMEM)
    return pl.pallas_call(
        kernel,
        in_specs=[vmem] * len(operands),
        out_specs=[vmem] * 3,
        out_shape=[
            jax.ShapeDtypeStruct(message, F32),
            jax.ShapeDtypeStruct(piece, F32),
            jax.ShapeDtypeStruct(piece, F32),
        ],
        scratch_shapes=[pltpu.VMEM(message, F32)] * 4
        + [
            pltpu.VMEM((pairs, planes, 2 * LANES), F32),
            pltpu.VMEM((comps, pairs, 2 * planes, 2 * LANES), F32),
            pltpu.VMEM((comps, pairs, 2, planes, 2 * LANES), F32),
        ]
        + [pltpu.VMEM(piece, F32)] * 5
        + [pltpu.VMEM(facts.shape, F32)] * 2
        + [
            pltpu.SemaphoreType.DMA((2, comps, count)),
            pltpu.SemaphoreType.DMA((2, comps, count)),
            pltpu.SemaphoreType.DMA((2 * comps + 1,)),
            pltpu.SemaphoreType.DMA((2 * comps + 1,)),
        ],
        compiler_params=pltpu.CompilerParams(
            vmem_limit_bytes=60 * 1024 * 1024, collective_id=0, has_side_effects=True
        ),
        name="advect_and_solve",
    )(*operands)


def recover_nodes(mid, mine, other, side, kind_lanes, weight_lanes, recover_cols, rows):
    comps, count, points, _ = mid.shape
    half = mine.shape[2]
    per = LANES // rows
    nodes = count * per * points
    second_at = recover_cols.shape[0] // 2

    def kernel(mid_ref, mine_ref, other_ref, side_ref, kinds, factor, weights, out):
        second = side_ref[0:1] > 0.5
        bit = lax.broadcasted_iota(jnp.int32, (4 * SUB, LANES), 1) // 8 % 2 == 0
        tiles = []
        for tile in range(half // LANES):
            at = slice(tile * LANES, (tile + 1) * LANES)
            first_half = mine_ref[0, :, at]
            last_half = other_ref[0, :, at]
            low_rows = jnp.where(second, last_half, first_half)
            high_rows = jnp.where(second, first_half, last_half)
            tiles.append(jnp.where(bit, low_rows, pltpu.roll(high_rows, 8, 1)))
            tiles.append(jnp.where(bit, pltpu.roll(low_rows, LANES - 8, 1), high_rows))
        both = mm(stacked_weights(weights[...]), stacked_values(jnp.concatenate(tiles, axis=1)))
        found = jnp.where(kinds[0:1] > 0.5, both[second_at : second_at + points], both[:points])
        for part in range(count):
            at = slice(part * LANES, (part + 1) * LANES)
            block = mid_ref[0, part] * factor[0:1, at] + found[:, at]
            block = jnp.concatenate([block, jnp.zeros((LANES - points, LANES), F32)], axis=0).T
            for local in range(per):
                start = (part * per + local) * points
                out[0, :, start : start + points] = block[local * rows : (local + 1) * rows, :points]

    piece = pl.BlockSpec((1, 4 * SUB, half), lambda c: (c, 0, 0))
    extra = (side, kind_lanes, weight_lanes, recover_cols)
    return pl.pallas_call(
        kernel,
        grid=(comps,),
        in_specs=[pl.BlockSpec((1, count, points, LANES), lambda c: (c, 0, 0, 0)), piece, piece]
        + [whole_spec(item.shape) for item in extra],
        out_specs=pl.BlockSpec((1, rows, nodes), lambda c: (c, 0, 0)),
        out_shape=jax.ShapeDtypeStruct((comps, rows, nodes), F32),
        compiler_params=params(),
        name="recover_nodes",
    )(mid, mine, other, *extra)


def edge_rows(matrix):
    shape = matrix.shape
    grouped = matrix.reshape(shape[0], 4, QUAD, shape[2])
    grouped = jnp.pad(grouped, ((0, 0), (0, 0), (0, SUB - QUAD), (0, 0)))
    return grouped.reshape(shape[0], 4 * SUB, shape[2])


def edge_cols(matrix):
    return edge_rows(matrix.swapaxes(1, 2)).swapaxes(1, 2)


def fast_device(
    velocity,
    geometry,
    element_kind,
    element_scale,
    dirichlet,
    schur_stiffness,
    schur_mass,
    lift,
    recover,
):
    count = lax.axis_size("planes")
    rows = velocity.shape[1]
    elems = element_kind.shape[0]
    points = QUAD * QUAD
    per = elems // count
    core = lax.axis_index("elem")
    place = lax.axis_index("planes")
    side = jnp.broadcast_to(core.astype(F32), (8, LANES))

    free = jnp.pad((1 - dirichlet).astype(F32), ((0, 0), (0, SUB - QUAD), (0, 0))).reshape(2 * SUB, elems)
    facts = jnp.concatenate(
        [free, (element_kind == 1).astype(F32)[None], element_scale[None], jnp.zeros((6, elems), F32)], axis=0
    )
    facts = facts.reshape(facts.shape[0], elems // 16, 2, 8).swapaxes(2, 3)
    facts = jnp.broadcast_to(facts[..., None], facts.shape + (8,)).reshape(facts.shape[0], elems * 8)

    def lam_of(row):
        return SIGMA_COEF + (BETA_COEF * ((row + 1) // 2).astype(F32)) ** 2

    lane = jnp.arange(count * LANES, dtype=jnp.int32)
    lam_half = lam_of(place * rows + core * 8 + lane % 8)
    lam_lanes = jnp.broadcast_to(lam_half[None], (8, lane.shape[0]))
    weight = SIGMA_COEF / (SIGMA_COEF + lam_of(place * rows + lane % rows))
    weight_lanes = jnp.broadcast_to(weight[None], (8, lane.shape[0]))
    kinds = jnp.broadcast_to((element_kind == 1).astype(F32)[None, :, None], (8, elems, rows)).reshape(8, elems * rows)
    geo = lax.dynamic_slice_in_dim(geometry.reshape(4, elems, points), place * per, per, 1)
    geo = jnp.pad(geo.swapaxes(0, 1), ((0, 0), (0, 4), (0, LANES - points)))

    lift_rows = edge_rows(lift).reshape(8 * SUB, points)
    matrices = jnp.concatenate([schur_stiffness, schur_mass], axis=0)
    matrices = edge_cols(edge_rows(matrices)).reshape(16 * SUB, 4 * SUB)
    recover_cols = jnp.pad(edge_cols(recover), ((0, 0), (0, 88 - points), (0, 0))).reshape(2 * 88, 4 * SUB)
    mid, mine, other = advect_and_solve(velocity, geo, lift_rows, kinds, side, facts, lam_lanes, matrices, count)
    return recover_nodes(mid, mine, other, side, kinds, weight_lanes, recover_cols, rows)


def per_device(velocity, geometry, element_kind, *rest):
    count = lax.axis_size("planes")
    rows = velocity.shape[1]
    elems = element_kind.shape[0]
    fits = rows == 16 and elems == LANES and elems * rows == count * LANES and lax.axis_size("elem") == 2
    body = fast_device if fits else plain_device
    return body(velocity, geometry, element_kind, *rest)


def solution(mesh):
    in_specs = (
        P(None, "planes", "elem"),
        P(None, "elem"),
        P("elem"),
        P("elem"),
        P(None, None, "elem"),
        P(),
        P(),
        P(),
        P(),
    )
    out_specs = P(None, "planes", "elem")
    return jax.shard_map(
        per_device, mesh=mesh, in_specs=in_specs, out_specs=out_specs, check_vma=False
    )
```

```python
import math

import jax
import jax.numpy as jnp
import numpy as np
from jax import lax
from jax.experimental import pallas as pl
from jax.experimental.pallas import tpu as pltpu
from jax.sharding import PartitionSpec as P

PLANES = 256
QUAD = 9
COLUMN_ELEMS = 32
CG_STEPS = 4


HIGHEST = lax.Precision.HIGHEST
SIGMA_COEF = 1.0
BETA_COEF = 0.01
STEP_DT = 0.002


def passed_along(value, axis, steps):
    count = lax.axis_size(axis)
    leading, last = (max(0, -steps), min(count, count - steps))
    return lax.ppermute(value, axis, [(source, source + steps) for source in range(leading, last)])


def gauss_derivative(points):
    nodes = -np.cos(np.pi * (2 * np.arange(points) + 1) / (2 * points))
    ident = np.eye(points)
    diffs = nodes[:, None] - nodes[None, :] + ident
    weights = 1.0 / np.prod(diffs, axis=1)
    matrix = weights[None, :] / weights[:, None] / diffs
    matrix = matrix * (1.0 - ident)
    return matrix - ident * matrix.sum(axis=1)[:, None]


def kron_tables():
    deriv = gauss_derivative(QUAD)
    identity = np.eye(QUAD)
    return (
        jnp.asarray(np.kron(deriv, identity), jnp.float32),
        jnp.asarray(np.kron(identity, deriv), jnp.float32),
    )


def fourier_tables(planes):
    zeta = jnp.arange(planes, dtype=jnp.int32)
    rows = jnp.arange(planes, dtype=jnp.int32)
    waves = (rows + 1) // 2
    phase = waves[None, :] * zeta[:, None] % planes
    angle = 2.0 * math.pi / planes * phase.astype(jnp.float32)
    cosine = jnp.cos(angle)
    sine = jnp.sin(angle)
    odd = (rows % 2 == 1)[None, :]
    first = (rows == 0)[None, :]
    last = (rows == planes - 1)[None, :]
    synth = jnp.where(first, 1.0, jnp.where(odd, cosine, sine))
    rate = BETA_COEF * waves.astype(jnp.float32)[None, :]
    slope = jnp.where(first | last, 0.0, jnp.where(odd, -rate * sine, rate * cosine))
    weight = jnp.where((rows == 0) | (rows == planes - 1), 1.0 / planes, 2.0 / planes).astype(
        jnp.float32
    )
    analysis = synth.T * weight[:, None]
    return (synth, slope, analysis)


def inner(first_pair, second_pair):
    return jnp.sum(first_pair[0] * second_pair[0], axis=(0, 2)) + jnp.sum(
        first_pair[1] * second_pair[1], axis=(0, 2)
    )


def global_total(first_pair, second_pair):
    return lax.psum(inner(first_pair, second_pair), "elem")


def global_squares(pair):
    return lax.psum(inner(pair, pair), "elem")


def assemble(outputs, incoming, free):
    left = outputs[:QUAD]
    right = outputs[QUAD : 2 * QUAD]
    bottom = outputs[2 * QUAD : 3 * QUAD]
    top = outputs[3 * QUAD :]
    vertical = left + jnp.concatenate([incoming, right[:, :, :-COLUMN_ELEMS]], axis=2)
    grid = top.reshape(top.shape[0], top.shape[1], -1, COLUMN_ELEMS)
    shifted = jnp.concatenate([jnp.zeros_like(grid[..., :1]), grid[..., :-1]], axis=3).reshape(
        bottom.shape
    )
    horizontal = bottom + shifted
    return (vertical * free[0], horizontal * free[1])


def plain_device(
    velocity,
    geometry,
    element_kind,
    element_scale,
    dirichlet,
    schur_stiffness,
    schur_mass,
    lift,
    recover,
):
    first, second = kron_tables()
    synth, slope, analysis = fourier_tables(PLANES)
    local_rows = velocity.shape[1]
    node_count = velocity.shape[2]
    share = node_count // lax.axis_size("planes")
    geo_part = lax.dynamic_slice_in_dim(geometry, lax.axis_index("planes") * share, share, 1)

    def transform(table, field):
        return jnp.einsum("zr,crm->czm", table, field, precision=HIGHEST)

    items = lax.all_to_all(velocity, "planes", split_axis=2, concat_axis=1, tiled=True)
    values = transform(synth, items)
    along_z = transform(slope, items)
    shaped = values.reshape(values.shape[:-1] + (-1, QUAD * QUAD))
    along_r = jnp.einsum("...en,mn->...em", shaped, first, precision=HIGHEST).reshape(values.shape)
    along_s = jnp.einsum("...en,mn->...em", shaped, second, precision=HIGHEST).reshape(values.shape)
    along_x = geo_part[0] * along_r + geo_part[1] * along_s
    along_y = geo_part[2] * along_r + geo_part[3] * along_s
    values, along_x, along_y, along_z = (values, along_x, along_y, along_z)
    advection = values[0] * along_x + values[1] * along_y + values[2] * along_z
    advection_hat = jnp.einsum("rz,czm->crm", analysis, advection, precision=HIGHEST)
    returned = lax.all_to_all(advection_hat, "planes", split_axis=1, concat_axis=2, tiled=True)
    intermediate = velocity - STEP_DT * returned
    elem_count = element_kind.shape[0]
    row_count = 3 * local_rows
    waves = (
        (lax.axis_index("planes") * local_rows + jnp.arange(local_rows, dtype=jnp.int32) + 1) // 2
    ).astype(jnp.float32)
    lam = jnp.tile(SIGMA_COEF + (BETA_COEF * waves) ** 2, 3)
    free = (1 - dirichlet).astype(jnp.float32)[:, :, None, :]
    chooser = (element_kind == 1).astype(jnp.float32)

    def element_apply(vector, kinds, scales):
        flat = vector.reshape(vector.shape[0], -1)
        results = []
        for kind in range(2):
            stiff = jnp.dot(schur_stiffness[kind], flat, precision=HIGHEST).reshape(vector.shape)
            massed = jnp.dot(schur_mass[kind], flat, precision=HIGHEST).reshape(vector.shape)
            results.append(stiff + lam[None, :, None] * massed)
        return scales[None, None, :] * jnp.where(kinds[None, None, :] > 0.5, results[1], results[0])

    def element_vector(vertical, horizontal):
        arriving = passed_along(vertical[:, :, :COLUMN_ELEMS], "elem", -1)
        right = jnp.concatenate([vertical[:, :, COLUMN_ELEMS:], arriving], axis=2)
        grid = horizontal.reshape(horizontal.shape[0], horizontal.shape[1], -1, COLUMN_ELEMS)
        top = jnp.concatenate([grid[..., 1:], jnp.zeros_like(grid[..., :1])], axis=3).reshape(
            horizontal.shape
        )
        return jnp.concatenate([vertical, right, horizontal, top], axis=0)

    node_values = (SIGMA_COEF * intermediate).reshape(row_count, elem_count, QUAD * QUAD)
    lifted = jnp.where(
        chooser[None, None, :] > 0.5,
        jnp.einsum("kn,ren->kre", lift[1], node_values, precision=HIGHEST),
        jnp.einsum("kn,ren->kre", lift[0], node_values, precision=HIGHEST),
    )
    lifted_right = passed_along(lifted[QUAD : 2 * QUAD, :, -COLUMN_ELEMS:], "elem", 1)
    forcing = assemble(lifted, lifted_right, free)
    trace = (jnp.zeros_like(forcing[0]), jnp.zeros_like(forcing[1]))
    residual = forcing
    direction = forcing
    norm_now = global_squares(residual)
    for sweep in range(CG_STEPS):
        outputs = element_apply(element_vector(direction[0], direction[1]), chooser, element_scale)
        operator_arriving = passed_along(outputs[QUAD : 2 * QUAD, :, -COLUMN_ELEMS:], "elem", 1)
        image = assemble(outputs, operator_arriving, free)
        alpha = (norm_now / global_total(direction, image))[None, :, None]
        trace = (trace[0] + alpha * direction[0], trace[1] + alpha * direction[1])
        residual = (residual[0] - alpha * image[0], residual[1] - alpha * image[1])
        norm_next = global_squares(residual)
        ratio = (norm_next / norm_now)[None, :, None]
        direction = (residual[0] + ratio * direction[0], residual[1] + ratio * direction[1])
        norm_now = norm_next
    vector = element_vector(trace[0], trace[1])
    recovered = jnp.where(
        chooser[None, :, None] > 0.5,
        jnp.einsum("nl,lre->ren", recover[1], vector, precision=HIGHEST),
        jnp.einsum("nl,lre->ren", recover[0], vector, precision=HIGHEST),
    )
    weight = SIGMA_COEF / (SIGMA_COEF + lam)
    result = (
        intermediate.reshape(row_count, elem_count, QUAD * QUAD) * weight[:, None, None] + recovered
    )
    return result.reshape(velocity.shape)


LANES = 128
SUB = 16
F32 = jnp.float32
BF16 = jnp.bfloat16


def split(value):
    high = value.astype(BF16)
    return high, (value - high.astype(F32)).astype(BF16)


def np_split(value):
    high = np.asarray(value, np.float32).astype(BF16)
    low = (np.asarray(value, np.float64) - high.astype(np.float64)).astype(np.float32).astype(BF16)
    return high, low


def mm(first, second):
    return jnp.dot(first, second, preferred_element_type=F32)


def stacked_weights(weights):
    high, low = split(weights)
    return jnp.concatenate([high, high, low], axis=1)


def stacked_values(values):
    high, low = split(values)
    return jnp.concatenate([high, low, high], axis=0)


def advect_tables(planes):
    zeta = np.arange(planes)
    rows = np.arange(planes)
    waves = (rows + 1) // 2
    angle = 2.0 * np.pi / planes * ((waves[None, :] * zeta[:, None]) % planes)
    odd = (rows % 2 == 1)[None, :]
    first = (rows == 0)[None, :]
    last = (rows == planes - 1)[None, :]
    synth = np.where(first, 1.0, np.where(odd, np.cos(angle), np.sin(angle)))
    rate = BETA_COEF * waves[None, :]
    slope = np.where(first | last, 0.0, np.where(odd, -rate * np.sin(angle), rate * np.cos(angle)))
    weight = np.where((rows == 0) | (rows == planes - 1), 1.0 / planes, 2.0 / planes)
    analysis = synth.T * weight[:, None]
    high, low = np_split(np.concatenate([synth, slope], axis=0))
    forward = np.concatenate([high, high, low], axis=1)
    high, low = np_split(analysis)
    backward = np.concatenate([high, high, low], axis=1)
    points = QUAD * QUAD
    deriv = gauss_derivative(QUAD)
    both = np.zeros((LANES, 2 * LANES))
    both[:points, :points] = np.kron(deriv, np.eye(QUAD)).T
    both[:points, LANES : LANES + points] = np.kron(np.eye(QUAD), deriv).T
    high, low = np_split(both)
    return jnp.asarray(forward), jnp.asarray(backward), jnp.asarray(np.concatenate([high, high, low], axis=0))


def whole_spec(shape):
    return pl.BlockSpec(shape, lambda *_: (0,) * len(shape))


def params():
    return pltpu.CompilerParams(vmem_limit_bytes=60 * 1024 * 1024)


def solve_rows(own, other, own_fact, other_fact, lam, side_row, weights):
    half = own.shape[1]
    wide = 2 * half
    column = COLUMN_ELEMS // SUB * LANES
    second = jnp.concatenate([side_row] * (half // LANES), axis=1) > 0.5

    def joined(first, last):
        return jnp.concatenate([jnp.where(second, last, first), jnp.where(second, first, last)], axis=1)

    facts = joined(own_fact, other_fact)
    free_v = facts[:SUB]
    free_h = facts[SUB : 2 * SUB]
    is_second = facts[2 * SUB : 2 * SUB + 1] > 0.5
    scale = facts[2 * SUB + 1 : 2 * SUB + 2]
    w_all = stacked_weights(weights)
    lane = lax.broadcasted_iota(jnp.int32, (1, wide), 1)
    along = lane % LANES // SUB
    odd_half = lane // 8 % 2 == 1
    tile = lane // LANES
    per_column = COLUMN_ELEMS // SUB
    top_edge = (tile % per_column == per_column - 1) & odd_half & (along == SUB // 2 - 1)
    low_edge = (tile % per_column == 0) & jnp.logical_not(odd_half) & (along == 0)

    def above(x):
        last = jnp.where(odd_half, pltpu.roll(x, wide - 8, 1), pltpu.roll(x, 104, 1))
        moved = jnp.where(along < SUB // 2 - 1, pltpu.roll(x, wide - 16, 1), last)
        return jnp.where(top_edge, 0.0, moved)

    def below(x):
        head = jnp.where(odd_half, pltpu.roll(x, wide - 104, 1), pltpu.roll(x, 8, 1))
        moved = jnp.where(along > 0, pltpu.roll(x, 16, 1), head)
        return jnp.where(low_edge, 0.0, moved)

    edge = jnp.zeros((SUB, column), F32)

    def vector_of(v, h):
        right = jnp.concatenate([v[:, column:], edge], axis=1)
        return jnp.concatenate([v, right, h, above(h)], axis=0)

    def gather(parts):
        right = jnp.concatenate([edge, parts[SUB : 2 * SUB, :-column]], axis=1)
        v = (parts[:SUB] + right) * free_v
        h = (parts[2 * SUB : 3 * SUB] + below(parts[3 * SUB :])) * free_h
        return v, h

    def total(product):
        acc = product[:, :LANES]
        for at in range(1, wide // LANES):
            acc = acc + product[:, at * LANES : (at + 1) * LANES]
        acc = jnp.sum(acc, axis=0, keepdims=True)
        acc = jnp.broadcast_to(acc, (8, LANES))
        for step in (8, 16, 32, 64):
            acc = acc + pltpu.roll(acc, step, 1)
        return acc[0:1]

    def spread(row):
        return jnp.concatenate([row] * (wide // LANES), axis=1)

    res_v, res_h = gather(joined(own, other))
    now = total(res_v * res_v + res_h * res_h)
    zero = jnp.zeros_like(res_v)

    def sweep(_, state):
        tr_v, tr_h, res_v, res_h, dir_v, dir_h, now = state
        both = mm(w_all, stacked_values(vector_of(dir_v, dir_h)))
        rows = 4 * SUB
        stiff = jnp.where(is_second, both[rows : 2 * rows], both[:rows])
        mass = jnp.where(is_second, both[3 * rows :], both[2 * rows : 3 * rows])
        im_v, im_h = gather(scale * (stiff + lam * mass))
        alpha = spread(now / total(dir_v * im_v + dir_h * im_h))
        tr_v, tr_h = tr_v + alpha * dir_v, tr_h + alpha * dir_h
        res_v, res_h = res_v - alpha * im_v, res_h - alpha * im_h
        fresh = total(res_v * res_v + res_h * res_h)
        ratio = spread(fresh / now)
        return tr_v, tr_h, res_v, res_h, res_v + ratio * dir_v, res_h + ratio * dir_h, fresh

    state = lax.fori_loop(0, CG_STEPS, sweep, (zero, zero, res_v, res_h, res_v, res_h, now))
    vector = vector_of(state[0], state[1])
    mine = jnp.where(second, vector[:, half:], vector[:, :half])
    away = jnp.where(second, vector[:, :half], vector[:, half:])
    return mine, away


def exact(first, second):
    return jnp.dot(first, second, precision=HIGHEST, preferred_element_type=F32)


def iota(shape, axis):
    return lax.broadcasted_iota(jnp.int32, shape, axis)


def lam_of(row):
    return SIGMA_COEF + (BETA_COEF * ((row + 1) // 2).astype(F32)) ** 2


def advect_and_solve(velocity, geometry, kind, scale, dirichlet, stiffness, mass, lift_maps, recover_maps, count):
    elems = kind.shape[1]
    comps, rows, nodes = velocity.shape
    points = QUAD * QUAD
    per = LANES // rows
    pairs = per // 2
    planes = count * rows
    half = count * LANES // 2
    forward, backward, deriv = advect_tables(planes)

    def kernel(
        vel_ref, geo_ref, kind_ref, scale_ref, fixed_ref, stiff_ref, mass_ref, lift_in, recover_in,
        forward_ref, backward_ref, deriv_ref,
        mid, mine_out, other_out, kinds, factor, recover_out, side_ref,
        sent, recv, hats, ret, store, fields, slopes, own, away, other, traces, their_traces, facts_out, their_facts,
        geo, lift_ref, mat_ref, lam_ref,
        send_sem, recv_sem, pair_send, pair_recv,
    ):
        me = lax.axis_index("planes")
        core = lax.axis_index("elem")
        barrier = pltpu.get_barrier_semaphore()

        def greet(step, carry):
            pl.semaphore_signal(
                barrier, inc=1, device_id={"planes": lax.rem(me + step, count)}, device_id_type=pl.DeviceIdType.MESH
            )
            return carry

        lax.fori_loop(1, count, greet, 0)
        pl.semaphore_signal(barrier, inc=1, device_id={"elem": 1 - core}, device_id_type=pl.DeviceIdType.MESH)

        def copy_to(source, target, way, comp, peer):
            return pltpu.make_async_remote_copy(
                src_ref=source.at[comp, peer],
                dst_ref=target.at[comp, me],
                send_sem=send_sem.at[way, comp, peer],
                recv_sem=recv_sem.at[way, comp, me],
                device_id={"planes": peer},
                device_id_type=pl.DeviceIdType.MESH,
            )

        def copy_from(source, target, way, comp, peer):
            return pltpu.make_async_remote_copy(
                src_ref=source.at[comp, peer],
                dst_ref=target.at[comp, peer],
                send_sem=send_sem.at[way, comp, peer],
                recv_sem=recv_sem.at[way, comp, peer],
                device_id={"planes": peer},
                device_id_type=pl.DeviceIdType.MESH,
            )

        def start_all(source, target, way, comp):
            def one(step, carry):
                copy_to(source, target, way, comp, lax.rem(me + count // 2 + step, count)).start()
                return carry

            lax.fori_loop(0, count // 2, one, 0)

            def two(step, carry):
                copy_to(source, target, way, comp, lax.rem(me + step, count)).start()
                return carry

            lax.fori_loop(1, count // 2, two, 0)

        def pair_copy(source, target, at):
            return pltpu.make_async_remote_copy(
                src_ref=source,
                dst_ref=target,
                send_sem=pair_send.at[at],
                recv_sem=pair_recv.at[at],
                device_id={"elem": 1 - core},
                device_id_type=pl.DeviceIdType.MESH,
            )

        def pack(comp):
            for part in range(count):
                pieces = []
                for local in range(per):
                    at = (part * per + local) * points
                    pieces.append(vel_ref[comp, :, at : at + points])
                sent[comp, part] = jnp.concatenate(pieces, axis=0).T

        def arrive(comp, part, block):
            block = jnp.concatenate([block, jnp.zeros((LANES - points, LANES), F32)], axis=0).T
            for local in range(per):
                at = local % 2 * LANES
                store[local // 2, pl.ds(pl.multiple_of(part * rows, rows), rows), at : at + LANES] = block[
                    local * rows : (local + 1) * rows
                ]

        def arrive_all(comp):
            arrive(comp, me, sent[comp, me])

            def one(step, carry):
                part = lax.rem(me + step, count)
                copy_from(sent, recv, 0, comp, part).wait_recv()
                arrive(comp, part, recv[comp, part])
                return carry

            lax.fori_loop(count // 2, count, one, 0)
            lax.fori_loop(1, count // 2, one, 0)

        def synthesize(comp):
            def one(pair, carry):
                fields[comp, pair] = mm(forward_ref[...], stacked_values(store[pair]))
                return carry

            lax.fori_loop(0, pairs, one, 0)

        def derive(comp):
            def one(pair, carry):
                for which in range(2):
                    high, low = split(fields[comp, pair, :planes, which * LANES : (which + 1) * LANES])
                    slopes[comp, pair, which] = mm(jnp.concatenate([high, low], axis=1), deriv_ref[: 2 * LANES]) + mm(
                        high, deriv_ref[2 * LANES :]
                    )
                return carry

            lax.fori_loop(0, pairs, one, 0)

        def advect(comp):
            def one(pair, carry):
                results = []
                for which in range(2):
                    at = slice(which * LANES, (which + 1) * LANES)
                    vel = [fields[item, pair, :planes, at] for item in range(comps)]
                    part = geo[pair * 2 + which]
                    results.append(
                        slopes[comp, pair, which, :, :LANES] * (vel[0] * part[0:1] + vel[1] * part[2:3])
                        + slopes[comp, pair, which, :, LANES:] * (vel[0] * part[1:2] + vel[1] * part[3:4])
                        + vel[2] * fields[comp, pair, planes:, at]
                    )
                store[pair] = mm(backward_ref[...], stacked_values(jnp.concatenate(results, axis=1)))
                return carry

            lax.fori_loop(0, pairs, one, 0)
            for part in range(count):
                block = jnp.concatenate(
                    [
                        store[local // 2, part * rows : (part + 1) * rows, local % 2 * LANES : (local % 2 + 1) * LANES]
                        for local in range(per)
                    ],
                    axis=0,
                )
                hats[comp, part] = block.T[:points]

        def lift(comp):
            def one(step, carry):
                copy_from(hats, ret, 1, comp, lax.rem(me + step, count)).wait_recv()
                return carry

            lax.fori_loop(1, count, one, 0)
            ret[comp, me] = hats[comp, me]
            for part in range(count):
                mid[comp, part] = sent[comp, part] - STEP_DT * ret[comp, part]
            field = jnp.concatenate([mid[comp, part] for part in range(count)], axis=1)
            high, low = split(SIGMA_COEF * field)
            w_high, w_low = split(lift_ref[...])
            both = mm(w_high, high) + (mm(w_high, low) + mm(w_low, high))
            lifted = jnp.where(kinds[0:1] > 0.5, both[4 * SUB :], both[: 4 * SUB])
            bit = lax.broadcasted_iota(jnp.int32, (4 * SUB, LANES), 1) // 8 % 2 == 0
            second = side_ref[0:1] > 0.5
            for tile in range(count // 2):
                even = lifted[:, 2 * tile * LANES : (2 * tile + 1) * LANES]
                odd = lifted[:, (2 * tile + 1) * LANES : (2 * tile + 2) * LANES]
                low_rows = jnp.where(bit, even, pltpu.roll(odd, 8, 1))
                high_rows = jnp.where(bit, pltpu.roll(even, LANES - 8, 1), odd)
                at = slice(tile * LANES, (tile + 1) * LANES)
                own[comp, :, at] = jnp.where(second, high_rows, low_rows)
                away[comp, :, at] = jnp.where(second, low_rows, high_rows)
            pair_copy(away.at[comp], other.at[comp], comp).start()

        def solve(comp):
            pair_copy(away.at[comp], other.at[comp], comp).wait_recv()
            mine, theirs = solve_rows(
                own[comp], other[comp], facts_out[...], their_facts[...], lam_ref[0:1], side_ref[0:1], mat_ref[...]
            )
            mine_out[comp] = mine
            traces[comp] = theirs
            pair_copy(traces.at[comp], their_traces.at[comp], comps + comp).start()

        def prepare():
            group = iota((4 * SUB, 4 * QUAD), 0)
            place = group // SUB * QUAD + group % SUB
            widen = ((place == iota((4 * SUB, 4 * QUAD), 1)) & (group % SUB < QUAD)).astype(F32)
            group = iota((4 * QUAD, 4 * SUB), 1)
            place = group // SUB * QUAD + group % SUB
            widen_cols = ((place == iota((4 * QUAD, 4 * SUB), 0)) & (group % SUB < QUAD)).astype(F32)
            recover_out[...] = jnp.zeros_like(recover_out)
            for which in range(2):
                at = which * 4 * SUB
                mat_ref[at : at + 4 * SUB] = exact(exact(widen, stiff_ref[:, which, :]), widen_cols)
                at = at + 8 * SUB
                mat_ref[at : at + 4 * SUB] = exact(exact(widen, mass_ref[:, which, :]), widen_cols)
                lift_ref[which * 4 * SUB : (which + 1) * 4 * SUB] = exact(widen, lift_in[:, which, :])
                recover_out[which * 88 : which * 88 + points] = exact(widen, recover_in[:, which, :]).T
            is_second = (kind_ref[...] == 1).astype(F32)
            pad = jnp.zeros((SUB - QUAD, elems), F32)
            free_v = (1 - fixed_ref[:, 0, :]).astype(F32)
            free_h = (1 - fixed_ref[:, 1, :]).astype(F32)
            table = jnp.concatenate(
                [free_v, pad, free_h, pad, is_second, scale_ref[...], jnp.zeros((6, elems), F32)], axis=0
            )
            lane = iota((elems, half), 1)
            element = lane // LANES * 16 + lane // 8 % 2 * 8 + lane % LANES // 16
            facts_out[...] = exact(table, (element == iota((elems, half), 0)).astype(F32))
            lane = iota((elems, 2 * half), 1)
            spread = (lane // rows == iota((elems, 2 * half), 0)).astype(F32)
            kinds[...] = exact(jnp.broadcast_to(is_second, (8, elems)), spread)
            lane = iota((8, 2 * half), 1)
            lam_ref[...] = lam_of(me * rows + core * 8 + lane % 8)
            factor[...] = SIGMA_COEF / (SIGMA_COEF + lam_of(me * rows + lane % rows))
            side_ref[...] = jnp.full((8, LANES), core, jnp.int32).astype(F32)
            geo[...] = jnp.zeros_like(geo)
            for part in range(count):

                @pl.when(me == part)
                def _():
                    for local in range(per):
                        at = (part * per + local) * points
                        geo[local, 0:4, 0:points] = geo_ref[:, at : at + points]

        pack(0)
        pl.semaphore_wait(barrier, count)
        start_all(sent, recv, 0, 0)
        for comp in range(1, comps):
            pack(comp)
            start_all(sent, recv, 0, comp)
        prepare()
        pair_copy(facts_out, their_facts, 2 * comps).start()
        for comp in range(comps):
            arrive_all(comp)
            synthesize(comp)
            if comp < comps - 1:
                derive(comp)
        for comp in range(comps):
            if comp == comps - 1:
                derive(comp)
            advect(comp)
            start_all(hats, ret, 1, comp)
        pair_copy(facts_out, their_facts, 2 * comps).wait_recv()
        for comp in range(comps):
            lift(comp)
            solve(comp)
        for comp in range(comps):
            pair_copy(traces.at[comp], their_traces.at[comp], comps + comp).wait_recv()
            other_out[comp] = their_traces[comp]
        pair_copy(facts_out, their_facts, 2 * comps).wait_send()
        for comp in range(comps):
            pair_copy(away.at[comp], other.at[comp], comp).wait_send()
            pair_copy(traces.at[comp], their_traces.at[comp], comps + comp).wait_send()

            def drain(step, carry):
                peer = lax.rem(me + step, count)
                copy_to(sent, recv, 0, comp, peer).wait_send()
                copy_to(hats, ret, 1, comp, peer).wait_send()
                return carry

            lax.fori_loop(1, count, drain, 0)

    message = (comps, count, points, LANES)
    piece = (comps, 4 * SUB, half)
    operands = (velocity, geometry, kind, scale, dirichlet, stiffness, mass, lift_maps, recover_maps)
    operands = operands + (forward, backward, deriv)
    facts = pltpu.VMEM((40, half), F32)
    vmem = pl.BlockSpec(memory_space=pltpu.VMEM)
    return pl.pallas_call(
        kernel,
        in_specs=[vmem] * len(operands),
        out_specs=[vmem] * 7,
        out_shape=[
            jax.ShapeDtypeStruct(message, F32),
            jax.ShapeDtypeStruct(piece, F32),
            jax.ShapeDtypeStruct(piece, F32),
            jax.ShapeDtypeStruct((8, 2 * half), F32),
            jax.ShapeDtypeStruct((8, 2 * half), F32),
            jax.ShapeDtypeStruct((2 * 88, 4 * SUB), F32),
            jax.ShapeDtypeStruct((8, LANES), F32),
        ],
        scratch_shapes=[pltpu.VMEM(message, F32)] * 4
        + [
            pltpu.VMEM((pairs, planes, 2 * LANES), F32),
            pltpu.VMEM((comps, pairs, 2 * planes, 2 * LANES), F32),
            pltpu.VMEM((comps, pairs, 2, planes, 2 * LANES), F32),
        ]
        + [pltpu.VMEM(piece, F32)] * 5
        + [
            facts,
            facts,
            pltpu.VMEM((per, 8, LANES), F32),
            pltpu.VMEM((8 * SUB, points), F32),
            pltpu.VMEM((16 * SUB, 4 * SUB), F32),
            pltpu.VMEM((8, 2 * half), F32),
        ]
        + [
            pltpu.SemaphoreType.DMA((2, comps, count)),
            pltpu.SemaphoreType.DMA((2, comps, count)),
            pltpu.SemaphoreType.DMA((2 * comps + 1,)),
            pltpu.SemaphoreType.DMA((2 * comps + 1,)),
        ],
        compiler_params=pltpu.CompilerParams(
            vmem_limit_bytes=60 * 1024 * 1024, collective_id=0, has_side_effects=True
        ),
        name="advect_and_solve",
    )(*operands)


def recover_nodes(mid, mine, other, side, kind_lanes, weight_lanes, recover_cols, rows):
    comps, count, points, _ = mid.shape
    half = mine.shape[2]
    per = LANES // rows
    nodes = count * per * points
    second_at = recover_cols.shape[0] // 2

    def kernel(mid_ref, mine_ref, other_ref, side_ref, kinds, factor, weights, out):
        second = side_ref[0:1] > 0.5
        bit = lax.broadcasted_iota(jnp.int32, (4 * SUB, LANES), 1) // 8 % 2 == 0
        tiles = []
        for tile in range(half // LANES):
            at = slice(tile * LANES, (tile + 1) * LANES)
            first_half = mine_ref[0, :, at]
            last_half = other_ref[0, :, at]
            low_rows = jnp.where(second, last_half, first_half)
            high_rows = jnp.where(second, first_half, last_half)
            tiles.append(jnp.where(bit, low_rows, pltpu.roll(high_rows, 8, 1)))
            tiles.append(jnp.where(bit, pltpu.roll(low_rows, LANES - 8, 1), high_rows))
        both = mm(stacked_weights(weights[...]), stacked_values(jnp.concatenate(tiles, axis=1)))
        found = jnp.where(kinds[0:1] > 0.5, both[second_at : second_at + points], both[:points])
        for part in range(count):
            at = slice(part * LANES, (part + 1) * LANES)
            block = mid_ref[0, part] * factor[0:1, at] + found[:, at]
            block = jnp.concatenate([block, jnp.zeros((LANES - points, LANES), F32)], axis=0).T
            for local in range(per):
                start = (part * per + local) * points
                out[0, :, start : start + points] = block[local * rows : (local + 1) * rows, :points]

    piece = pl.BlockSpec((1, 4 * SUB, half), lambda c: (c, 0, 0))
    extra = (side, kind_lanes, weight_lanes, recover_cols)
    return pl.pallas_call(
        kernel,
        grid=(comps,),
        in_specs=[pl.BlockSpec((1, count, points, LANES), lambda c: (c, 0, 0, 0)), piece, piece]
        + [whole_spec(item.shape) for item in extra],
        out_specs=pl.BlockSpec((1, rows, nodes), lambda c: (c, 0, 0)),
        out_shape=jax.ShapeDtypeStruct((comps, rows, nodes), F32),
        compiler_params=params(),
        name="recover_nodes",
    )(mid, mine, other, *extra)


def fast_device(
    velocity,
    geometry,
    element_kind,
    element_scale,
    dirichlet,
    schur_stiffness,
    schur_mass,
    lift,
    recover,
):
    count = lax.axis_size("planes")
    mid, mine, other, kinds, factor, recover_cols, side = advect_and_solve(
        velocity,
        geometry,
        element_kind[None],
        element_scale[None],
        dirichlet.swapaxes(0, 1),
        schur_stiffness.swapaxes(0, 1),
        schur_mass.swapaxes(0, 1),
        lift.swapaxes(0, 1),
        recover.transpose(2, 0, 1),
        count,
    )
    return recover_nodes(mid, mine, other, side, kinds, factor, recover_cols, velocity.shape[1])


def per_device(velocity, geometry, element_kind, *rest):
    count = lax.axis_size("planes")
    rows = velocity.shape[1]
    elems = element_kind.shape[0]
    fits = rows == 16 and elems == LANES and elems * rows == count * LANES and lax.axis_size("elem") == 2
    body = fast_device if fits else plain_device
    return body(velocity, geometry, element_kind, *rest)


def solution(mesh):
    in_specs = (
        P(None, "planes", "elem"),
        P(None, "elem"),
        P("elem"),
        P("elem"),
        P(None, None, "elem"),
        P(),
        P(),
        P(),
        P(),
    )
    out_specs = P(None, "planes", "elem")
    return jax.shard_map(
        per_device, mesh=mesh, in_specs=in_specs, out_specs=out_specs, check_vma=False
    )
```

```python
import math

import jax
import jax.numpy as jnp
import numpy as np
from jax import lax
from jax.experimental import pallas as pl
from jax.experimental.pallas import tpu as pltpu
from jax.sharding import PartitionSpec as P

PLANES = 256
QUAD = 9
COLUMN_ELEMS = 32
CG_STEPS = 4


HIGHEST = lax.Precision.HIGHEST
SIGMA_COEF = 1.0
BETA_COEF = 0.01
STEP_DT = 0.002


def passed_along(value, axis, steps):
    count = lax.axis_size(axis)
    leading, last = (max(0, -steps), min(count, count - steps))
    return lax.ppermute(value, axis, [(source, source + steps) for source in range(leading, last)])


def gauss_derivative(points):
    nodes = -np.cos(np.pi * (2 * np.arange(points) + 1) / (2 * points))
    ident = np.eye(points)
    diffs = nodes[:, None] - nodes[None, :] + ident
    weights = 1.0 / np.prod(diffs, axis=1)
    matrix = weights[None, :] / weights[:, None] / diffs
    matrix = matrix * (1.0 - ident)
    return matrix - ident * matrix.sum(axis=1)[:, None]


def kron_tables():
    deriv = gauss_derivative(QUAD)
    identity = np.eye(QUAD)
    return (
        jnp.asarray(np.kron(deriv, identity), jnp.float32),
        jnp.asarray(np.kron(identity, deriv), jnp.float32),
    )


def fourier_tables(planes):
    zeta = jnp.arange(planes, dtype=jnp.int32)
    rows = jnp.arange(planes, dtype=jnp.int32)
    waves = (rows + 1) // 2
    phase = waves[None, :] * zeta[:, None] % planes
    angle = 2.0 * math.pi / planes * phase.astype(jnp.float32)
    cosine = jnp.cos(angle)
    sine = jnp.sin(angle)
    odd = (rows % 2 == 1)[None, :]
    first = (rows == 0)[None, :]
    last = (rows == planes - 1)[None, :]
    synth = jnp.where(first, 1.0, jnp.where(odd, cosine, sine))
    rate = BETA_COEF * waves.astype(jnp.float32)[None, :]
    slope = jnp.where(first | last, 0.0, jnp.where(odd, -rate * sine, rate * cosine))
    weight = jnp.where((rows == 0) | (rows == planes - 1), 1.0 / planes, 2.0 / planes).astype(
        jnp.float32
    )
    analysis = synth.T * weight[:, None]
    return (synth, slope, analysis)


def inner(first_pair, second_pair):
    return jnp.sum(first_pair[0] * second_pair[0], axis=(0, 2)) + jnp.sum(
        first_pair[1] * second_pair[1], axis=(0, 2)
    )


def global_total(first_pair, second_pair):
    return lax.psum(inner(first_pair, second_pair), "elem")


def global_squares(pair):
    return lax.psum(inner(pair, pair), "elem")


def assemble(outputs, incoming, free):
    left = outputs[:QUAD]
    right = outputs[QUAD : 2 * QUAD]
    bottom = outputs[2 * QUAD : 3 * QUAD]
    top = outputs[3 * QUAD :]
    vertical = left + jnp.concatenate([incoming, right[:, :, :-COLUMN_ELEMS]], axis=2)
    grid = top.reshape(top.shape[0], top.shape[1], -1, COLUMN_ELEMS)
    shifted = jnp.concatenate([jnp.zeros_like(grid[..., :1]), grid[..., :-1]], axis=3).reshape(
        bottom.shape
    )
    horizontal = bottom + shifted
    return (vertical * free[0], horizontal * free[1])


def plain_device(
    velocity,
    geometry,
    element_kind,
    element_scale,
    dirichlet,
    schur_stiffness,
    schur_mass,
    lift,
    recover,
):
    first, second = kron_tables()
    synth, slope, analysis = fourier_tables(PLANES)
    local_rows = velocity.shape[1]
    node_count = velocity.shape[2]
    share = node_count // lax.axis_size("planes")
    geo_part = lax.dynamic_slice_in_dim(geometry, lax.axis_index("planes") * share, share, 1)

    def transform(table, field):
        return jnp.einsum("zr,crm->czm", table, field, precision=HIGHEST)

    items = lax.all_to_all(velocity, "planes", split_axis=2, concat_axis=1, tiled=True)
    values = transform(synth, items)
    along_z = transform(slope, items)
    shaped = values.reshape(values.shape[:-1] + (-1, QUAD * QUAD))
    along_r = jnp.einsum("...en,mn->...em", shaped, first, precision=HIGHEST).reshape(values.shape)
    along_s = jnp.einsum("...en,mn->...em", shaped, second, precision=HIGHEST).reshape(values.shape)
    along_x = geo_part[0] * along_r + geo_part[1] * along_s
    along_y = geo_part[2] * along_r + geo_part[3] * along_s
    values, along_x, along_y, along_z = (values, along_x, along_y, along_z)
    advection = values[0] * along_x + values[1] * along_y + values[2] * along_z
    advection_hat = jnp.einsum("rz,czm->crm", analysis, advection, precision=HIGHEST)
    returned = lax.all_to_all(advection_hat, "planes", split_axis=1, concat_axis=2, tiled=True)
    intermediate = velocity - STEP_DT * returned
    elem_count = element_kind.shape[0]
    row_count = 3 * local_rows
    waves = (
        (lax.axis_index("planes") * local_rows + jnp.arange(local_rows, dtype=jnp.int32) + 1) // 2
    ).astype(jnp.float32)
    lam = jnp.tile(SIGMA_COEF + (BETA_COEF * waves) ** 2, 3)
    free = (1 - dirichlet).astype(jnp.float32)[:, :, None, :]
    chooser = (element_kind == 1).astype(jnp.float32)

    def element_apply(vector, kinds, scales):
        flat = vector.reshape(vector.shape[0], -1)
        results = []
        for kind in range(2):
            stiff = jnp.dot(schur_stiffness[kind], flat, precision=HIGHEST).reshape(vector.shape)
            massed = jnp.dot(schur_mass[kind], flat, precision=HIGHEST).reshape(vector.shape)
            results.append(stiff + lam[None, :, None] * massed)
        return scales[None, None, :] * jnp.where(kinds[None, None, :] > 0.5, results[1], results[0])

    def element_vector(vertical, horizontal):
        arriving = passed_along(vertical[:, :, :COLUMN_ELEMS], "elem", -1)
        right = jnp.concatenate([vertical[:, :, COLUMN_ELEMS:], arriving], axis=2)
        grid = horizontal.reshape(horizontal.shape[0], horizontal.shape[1], -1, COLUMN_ELEMS)
        top = jnp.concatenate([grid[..., 1:], jnp.zeros_like(grid[..., :1])], axis=3).reshape(
            horizontal.shape
        )
        return jnp.concatenate([vertical, right, horizontal, top], axis=0)

    node_values = (SIGMA_COEF * intermediate).reshape(row_count, elem_count, QUAD * QUAD)
    lifted = jnp.where(
        chooser[None, None, :] > 0.5,
        jnp.einsum("kn,ren->kre", lift[1], node_values, precision=HIGHEST),
        jnp.einsum("kn,ren->kre", lift[0], node_values, precision=HIGHEST),
    )
    lifted_right = passed_along(lifted[QUAD : 2 * QUAD, :, -COLUMN_ELEMS:], "elem", 1)
    forcing = assemble(lifted, lifted_right, free)
    trace = (jnp.zeros_like(forcing[0]), jnp.zeros_like(forcing[1]))
    residual = forcing
    direction = forcing
    norm_now = global_squares(residual)
    for sweep in range(CG_STEPS):
        outputs = element_apply(element_vector(direction[0], direction[1]), chooser, element_scale)
        operator_arriving = passed_along(outputs[QUAD : 2 * QUAD, :, -COLUMN_ELEMS:], "elem", 1)
        image = assemble(outputs, operator_arriving, free)
        alpha = (norm_now / global_total(direction, image))[None, :, None]
        trace = (trace[0] + alpha * direction[0], trace[1] + alpha * direction[1])
        residual = (residual[0] - alpha * image[0], residual[1] - alpha * image[1])
        norm_next = global_squares(residual)
        ratio = (norm_next / norm_now)[None, :, None]
        direction = (residual[0] + ratio * direction[0], residual[1] + ratio * direction[1])
        norm_now = norm_next
    vector = element_vector(trace[0], trace[1])
    recovered = jnp.where(
        chooser[None, :, None] > 0.5,
        jnp.einsum("nl,lre->ren", recover[1], vector, precision=HIGHEST),
        jnp.einsum("nl,lre->ren", recover[0], vector, precision=HIGHEST),
    )
    weight = SIGMA_COEF / (SIGMA_COEF + lam)
    result = (
        intermediate.reshape(row_count, elem_count, QUAD * QUAD) * weight[:, None, None] + recovered
    )
    return result.reshape(velocity.shape)


LANES = 128
SUB = 16
F32 = jnp.float32
BF16 = jnp.bfloat16


def split(value):
    high = value.astype(BF16)
    return high, (value - high.astype(F32)).astype(BF16)


def np_split(value):
    high = np.asarray(value, np.float32).astype(BF16)
    low = (np.asarray(value, np.float64) - high.astype(np.float64)).astype(np.float32).astype(BF16)
    return high, low


def mm(first, second):
    return jnp.dot(first, second, preferred_element_type=F32)


def stacked_weights(weights):
    high, low = split(weights)
    return jnp.concatenate([high, high, low], axis=1)


def stacked_values(values):
    high, low = split(values)
    return jnp.concatenate([high, low, high], axis=0)


def advect_tables(planes):
    zeta = np.arange(planes)
    rows = np.arange(planes)
    waves = (rows + 1) // 2
    angle = 2.0 * np.pi / planes * ((waves[None, :] * zeta[:, None]) % planes)
    odd = (rows % 2 == 1)[None, :]
    first = (rows == 0)[None, :]
    last = (rows == planes - 1)[None, :]
    synth = np.where(first, 1.0, np.where(odd, np.cos(angle), np.sin(angle)))
    rate = BETA_COEF * waves[None, :]
    slope = np.where(first | last, 0.0, np.where(odd, -rate * np.sin(angle), rate * np.cos(angle)))
    weight = np.where((rows == 0) | (rows == planes - 1), 1.0 / planes, 2.0 / planes)
    analysis = synth.T * weight[:, None]
    high, low = np_split(np.concatenate([synth, slope], axis=0))
    forward = np.concatenate([high, high, low], axis=1)
    high, low = np_split(analysis)
    backward = np.concatenate([high, high, low], axis=1)
    points = QUAD * QUAD
    deriv = gauss_derivative(QUAD)
    both = np.zeros((LANES, 2 * LANES))
    both[:points, :points] = np.kron(deriv, np.eye(QUAD)).T
    both[:points, LANES : LANES + points] = np.kron(np.eye(QUAD), deriv).T
    high, low = np_split(both)
    return jnp.asarray(forward), jnp.asarray(backward), jnp.asarray(np.concatenate([high, high, low], axis=0))


def whole_spec(shape):
    return pl.BlockSpec(shape, lambda *_: (0,) * len(shape))


def params():
    return pltpu.CompilerParams(vmem_limit_bytes=60 * 1024 * 1024)


def solve_rows(own, other, own_fact, other_fact, lam, side_row, weights):
    half = own.shape[1]
    wide = 2 * half
    column = COLUMN_ELEMS // SUB * LANES
    second = jnp.concatenate([side_row] * (half // LANES), axis=1) > 0.5

    def joined(first, last):
        return jnp.concatenate([jnp.where(second, last, first), jnp.where(second, first, last)], axis=1)

    facts = joined(own_fact, other_fact)
    free_v = facts[:SUB]
    free_h = facts[SUB : 2 * SUB]
    is_second = facts[2 * SUB : 2 * SUB + 1] > 0.5
    scale = facts[2 * SUB + 1 : 2 * SUB + 2]
    w_all = stacked_weights(weights)
    lane = lax.broadcasted_iota(jnp.int32, (1, wide), 1)
    along = lane % LANES // SUB
    odd_half = lane // 8 % 2 == 1
    tile = lane // LANES
    per_column = COLUMN_ELEMS // SUB
    top_edge = (tile % per_column == per_column - 1) & odd_half & (along == SUB // 2 - 1)
    low_edge = (tile % per_column == 0) & jnp.logical_not(odd_half) & (along == 0)

    def above(x):
        last = jnp.where(odd_half, pltpu.roll(x, wide - 8, 1), pltpu.roll(x, 104, 1))
        moved = jnp.where(along < SUB // 2 - 1, pltpu.roll(x, wide - 16, 1), last)
        return jnp.where(top_edge, 0.0, moved)

    def below(x):
        head = jnp.where(odd_half, pltpu.roll(x, wide - 104, 1), pltpu.roll(x, 8, 1))
        moved = jnp.where(along > 0, pltpu.roll(x, 16, 1), head)
        return jnp.where(low_edge, 0.0, moved)

    edge = jnp.zeros((SUB, column), F32)

    def vector_of(v, h):
        right = jnp.concatenate([v[:, column:], edge], axis=1)
        return jnp.concatenate([v, right, h, above(h)], axis=0)

    def gather(parts):
        right = jnp.concatenate([edge, parts[SUB : 2 * SUB, :-column]], axis=1)
        v = (parts[:SUB] + right) * free_v
        h = (parts[2 * SUB : 3 * SUB] + below(parts[3 * SUB :])) * free_h
        return v, h

    def total(product):
        acc = product[:, :LANES]
        for at in range(1, wide // LANES):
            acc = acc + product[:, at * LANES : (at + 1) * LANES]
        acc = jnp.sum(acc, axis=0, keepdims=True)
        acc = jnp.broadcast_to(acc, (8, LANES))
        for step in (8, 16, 32, 64):
            acc = acc + pltpu.roll(acc, step, 1)
        return acc[0:1]

    def spread(row):
        return jnp.concatenate([row] * (wide // LANES), axis=1)

    res_v, res_h = gather(joined(own, other))
    now = total(res_v * res_v + res_h * res_h)
    zero = jnp.zeros_like(res_v)

    def sweep(_, state):
        tr_v, tr_h, res_v, res_h, dir_v, dir_h, now = state
        both = mm(w_all, stacked_values(vector_of(dir_v, dir_h)))
        rows = 4 * SUB
        stiff = jnp.where(is_second, both[rows : 2 * rows], both[:rows])
        mass = jnp.where(is_second, both[3 * rows :], both[2 * rows : 3 * rows])
        im_v, im_h = gather(scale * (stiff + lam * mass))
        alpha = spread(now / total(dir_v * im_v + dir_h * im_h))
        tr_v, tr_h = tr_v + alpha * dir_v, tr_h + alpha * dir_h
        res_v, res_h = res_v - alpha * im_v, res_h - alpha * im_h
        fresh = total(res_v * res_v + res_h * res_h)
        ratio = spread(fresh / now)
        return tr_v, tr_h, res_v, res_h, res_v + ratio * dir_v, res_h + ratio * dir_h, fresh

    state = lax.fori_loop(0, CG_STEPS, sweep, (zero, zero, res_v, res_h, res_v, res_h, now))
    vector = vector_of(state[0], state[1])
    mine = jnp.where(second, vector[:, half:], vector[:, :half])
    away = jnp.where(second, vector[:, :half], vector[:, half:])
    return mine, away


def exact(first, second):
    return jnp.dot(first, second, precision=HIGHEST, preferred_element_type=F32)


def iota(shape, axis):
    return lax.broadcasted_iota(jnp.int32, shape, axis)


def lam_of(row):
    return SIGMA_COEF + (BETA_COEF * ((row + 1) // 2).astype(F32)) ** 2


def advect_and_solve(velocity, geometry, kind, scale, dirichlet, stiffness, mass, lift_maps, recover_maps, count):
    elems = kind.shape[1]
    comps, rows, nodes = velocity.shape
    points = QUAD * QUAD
    per = LANES // rows
    pairs = per // 2
    planes = count * rows
    half = count * LANES // 2
    forward, backward, deriv = advect_tables(planes)

    def kernel(
        vel_ref, geo_ref, kind_ref, scale_ref, fixed_ref, stiff_ref, mass_ref, lift_in, recover_in,
        forward_ref, backward_ref, deriv_ref,
        mid, mine_out, other_out, kinds, factor, recover_out, side_ref,
        sent, recv, hats, ret, store, fields, slopes, own, away, other, traces, their_traces, facts_out, their_facts,
        geo, lift_ref, mat_ref, lam_ref,
        send_sem, recv_sem, pair_send, pair_recv,
    ):
        me = lax.axis_index("planes")
        core = lax.axis_index("elem")
        barrier = pltpu.get_barrier_semaphore()

        def peer_at(step):
            bits = count.bit_length() - 1
            peer = 0
            for bit in range(bits):
                weight = count // 2 // 2**bit
                peer = peer + weight * ((me // weight + step // 2**bit) % 2)
            return peer

        def greet(step, carry):
            pl.semaphore_signal(
                barrier, inc=1, device_id={"planes": peer_at(step)}, device_id_type=pl.DeviceIdType.MESH
            )
            return carry

        lax.fori_loop(1, count, greet, 0)
        pl.semaphore_signal(barrier, inc=1, device_id={"elem": 1 - core}, device_id_type=pl.DeviceIdType.MESH)

        def copy_to(source, target, way, comp, peer):
            return pltpu.make_async_remote_copy(
                src_ref=source.at[comp, peer],
                dst_ref=target.at[comp, me],
                send_sem=send_sem.at[way, comp, peer],
                recv_sem=recv_sem.at[way, comp, me],
                device_id={"planes": peer},
                device_id_type=pl.DeviceIdType.MESH,
            )

        def copy_from(source, target, way, comp, peer):
            return pltpu.make_async_remote_copy(
                src_ref=source.at[comp, peer],
                dst_ref=target.at[comp, peer],
                send_sem=send_sem.at[way, comp, peer],
                recv_sem=recv_sem.at[way, comp, peer],
                device_id={"planes": peer},
                device_id_type=pl.DeviceIdType.MESH,
            )

        def start_all(source, target, way, comp):
            def one(step, carry):
                copy_to(source, target, way, comp, peer_at(step)).start()
                return carry

            lax.fori_loop(1, count, one, 0)

        def pair_copy(source, target, at):
            return pltpu.make_async_remote_copy(
                src_ref=source,
                dst_ref=target,
                send_sem=pair_send.at[at],
                recv_sem=pair_recv.at[at],
                device_id={"elem": 1 - core},
                device_id_type=pl.DeviceIdType.MESH,
            )

        def pack(comp):
            for part in range(count):
                pieces = []
                for local in range(per):
                    at = (part * per + local) * points
                    pieces.append(vel_ref[comp, :, at : at + points])
                sent[comp, part] = jnp.concatenate(pieces, axis=0).T

        def arrive(comp, part, block):
            block = jnp.concatenate([block, jnp.zeros((LANES - points, LANES), F32)], axis=0).T
            for local in range(per):
                at = local % 2 * LANES
                store[local // 2, pl.ds(pl.multiple_of(part * rows, rows), rows), at : at + LANES] = block[
                    local * rows : (local + 1) * rows
                ]

        def arrive_all(comp):
            arrive(comp, me, sent[comp, me])

            def one(step, carry):
                part = peer_at(step)
                copy_from(sent, recv, 0, comp, part).wait_recv()
                arrive(comp, part, recv[comp, part])
                return carry

            lax.fori_loop(1, count, one, 0)

        def synthesize(comp):
            def one(pair, carry):
                fields[comp, pair] = mm(forward_ref[...], stacked_values(store[pair]))
                return carry

            lax.fori_loop(0, pairs, one, 0)

        def derive(comp):
            def one(pair, carry):
                for which in range(2):
                    high, low = split(fields[comp, pair, :planes, which * LANES : (which + 1) * LANES])
                    slopes[comp, pair, which] = mm(jnp.concatenate([high, low], axis=1), deriv_ref[: 2 * LANES]) + mm(
                        high, deriv_ref[2 * LANES :]
                    )
                return carry

            lax.fori_loop(0, pairs, one, 0)

        def advect(comp):
            def one(pair, carry):
                results = []
                for which in range(2):
                    at = slice(which * LANES, (which + 1) * LANES)
                    vel = [fields[item, pair, :planes, at] for item in range(comps)]
                    part = geo[pair * 2 + which]
                    results.append(
                        slopes[comp, pair, which, :, :LANES] * (vel[0] * part[0:1] + vel[1] * part[2:3])
                        + slopes[comp, pair, which, :, LANES:] * (vel[0] * part[1:2] + vel[1] * part[3:4])
                        + vel[2] * fields[comp, pair, planes:, at]
                    )
                store[pair] = mm(backward_ref[...], stacked_values(jnp.concatenate(results, axis=1)))
                return carry

            lax.fori_loop(0, pairs, one, 0)
            for part in range(count):
                block = jnp.concatenate(
                    [
                        store[local // 2, part * rows : (part + 1) * rows, local % 2 * LANES : (local % 2 + 1) * LANES]
                        for local in range(per)
                    ],
                    axis=0,
                )
                hats[comp, part] = block.T[:points]

        def lift(comp):
            def one(step, carry):
                copy_from(hats, ret, 1, comp, peer_at(step)).wait_recv()
                return carry

            lax.fori_loop(1, count, one, 0)
            ret[comp, me] = hats[comp, me]
            for part in range(count):
                mid[comp, part] = sent[comp, part] - STEP_DT * ret[comp, part]
            field = jnp.concatenate([mid[comp, part] for part in range(count)], axis=1)
            high, low = split(SIGMA_COEF * field)
            w_high, w_low = split(lift_ref[...])
            both = mm(w_high, high) + (mm(w_high, low) + mm(w_low, high))
            lifted = jnp.where(kinds[0:1] > 0.5, both[4 * SUB :], both[: 4 * SUB])
            bit = lax.broadcasted_iota(jnp.int32, (4 * SUB, LANES), 1) // 8 % 2 == 0
            second = side_ref[0:1] > 0.5
            for tile in range(count // 2):
                even = lifted[:, 2 * tile * LANES : (2 * tile + 1) * LANES]
                odd = lifted[:, (2 * tile + 1) * LANES : (2 * tile + 2) * LANES]
                low_rows = jnp.where(bit, even, pltpu.roll(odd, 8, 1))
                high_rows = jnp.where(bit, pltpu.roll(even, LANES - 8, 1), odd)
                at = slice(tile * LANES, (tile + 1) * LANES)
                own[comp, :, at] = jnp.where(second, high_rows, low_rows)
                away[comp, :, at] = jnp.where(second, low_rows, high_rows)
            pair_copy(away.at[comp], other.at[comp], comp).start()

        def solve(comp):
            pair_copy(away.at[comp], other.at[comp], comp).wait_recv()
            mine, theirs = solve_rows(
                own[comp], other[comp], facts_out[...], their_facts[...], lam_ref[0:1], side_ref[0:1], mat_ref[...]
            )
            mine_out[comp] = mine
            traces[comp] = theirs
            pair_copy(traces.at[comp], their_traces.at[comp], comps + comp).start()

        def prepare():
            group = iota((4 * SUB, 4 * QUAD), 0)
            place = group // SUB * QUAD + group % SUB
            widen = ((place == iota((4 * SUB, 4 * QUAD), 1)) & (group % SUB < QUAD)).astype(F32)
            group = iota((4 * QUAD, 4 * SUB), 1)
            place = group // SUB * QUAD + group % SUB
            widen_cols = ((place == iota((4 * QUAD, 4 * SUB), 0)) & (group % SUB < QUAD)).astype(F32)
            recover_out[...] = jnp.zeros_like(recover_out)
            for which in range(2):
                at = which * 4 * SUB
                mat_ref[at : at + 4 * SUB] = exact(exact(widen, stiff_ref[:, which, :]), widen_cols)
                at = at + 8 * SUB
                mat_ref[at : at + 4 * SUB] = exact(exact(widen, mass_ref[:, which, :]), widen_cols)
                lift_ref[which * 4 * SUB : (which + 1) * 4 * SUB] = exact(widen, lift_in[:, which, :])
                recover_out[which * 88 : which * 88 + points] = exact(widen, recover_in[:, which, :]).T
            is_second = (kind_ref[...] == 1).astype(F32)
            pad = jnp.zeros((SUB - QUAD, elems), F32)
            free_v = (1 - fixed_ref[:, 0, :]).astype(F32)
            free_h = (1 - fixed_ref[:, 1, :]).astype(F32)
            table = jnp.concatenate(
                [free_v, pad, free_h, pad, is_second, scale_ref[...], jnp.zeros((6, elems), F32)], axis=0
            )
            lane = iota((elems, half), 1)
            element = lane // LANES * 16 + lane // 8 % 2 * 8 + lane % LANES // 16
            facts_out[...] = exact(table, (element == iota((elems, half), 0)).astype(F32))
            lane = iota((elems, 2 * half), 1)
            spread = (lane // rows == iota((elems, 2 * half), 0)).astype(F32)
            kinds[...] = exact(jnp.broadcast_to(is_second, (8, elems)), spread)
            lane = iota((8, 2 * half), 1)
            lam_ref[...] = lam_of(me * rows + core * 8 + lane % 8)
            factor[...] = SIGMA_COEF / (SIGMA_COEF + lam_of(me * rows + lane % rows))
            side_ref[...] = jnp.full((8, LANES), core, jnp.int32).astype(F32)
            geo[...] = jnp.zeros_like(geo)
            for part in range(count):

                @pl.when(me == part)
                def _():
                    for local in range(per):
                        at = (part * per + local) * points
                        geo[local, 0:4, 0:points] = geo_ref[:, at : at + points]

        pack(0)
        pl.semaphore_wait(barrier, count)
        start_all(sent, recv, 0, 0)
        for comp in range(1, comps):
            pack(comp)
            start_all(sent, recv, 0, comp)
        prepare()
        pair_copy(facts_out, their_facts, 2 * comps).start()
        for comp in range(comps):
            arrive_all(comp)
            synthesize(comp)
            if comp < comps - 1:
                derive(comp)
        for comp in range(comps):
            if comp == comps - 1:
                derive(comp)
            advect(comp)
            start_all(hats, ret, 1, comp)
        pair_copy(facts_out, their_facts, 2 * comps).wait_recv()
        for comp in range(comps):
            lift(comp)
            solve(comp)
        for comp in range(comps):
            pair_copy(traces.at[comp], their_traces.at[comp], comps + comp).wait_recv()
            other_out[comp] = their_traces[comp]
        pair_copy(facts_out, their_facts, 2 * comps).wait_send()
        for comp in range(comps):
            pair_copy(away.at[comp], other.at[comp], comp).wait_send()
            pair_copy(traces.at[comp], their_traces.at[comp], comps + comp).wait_send()

            def drain(step, carry):
                peer = peer_at(step)
                copy_to(sent, recv, 0, comp, peer).wait_send()
                copy_to(hats, ret, 1, comp, peer).wait_send()
                return carry

            lax.fori_loop(1, count, drain, 0)

    message = (comps, count, points, LANES)
    piece = (comps, 4 * SUB, half)
    operands = (velocity, geometry, kind, scale, dirichlet, stiffness, mass, lift_maps, recover_maps)
    operands = operands + (forward, backward, deriv)
    facts = pltpu.VMEM((40, half), F32)
    vmem = pl.BlockSpec(memory_space=pltpu.VMEM)
    return pl.pallas_call(
        kernel,
        in_specs=[vmem] * len(operands),
        out_specs=[vmem] * 7,
        out_shape=[
            jax.ShapeDtypeStruct(message, F32),
            jax.ShapeDtypeStruct(piece, F32),
            jax.ShapeDtypeStruct(piece, F32),
            jax.ShapeDtypeStruct((8, 2 * half), F32),
            jax.ShapeDtypeStruct((8, 2 * half), F32),
            jax.ShapeDtypeStruct((2 * 88, 4 * SUB), F32),
            jax.ShapeDtypeStruct((8, LANES), F32),
        ],
        scratch_shapes=[pltpu.VMEM(message, F32)] * 4
        + [
            pltpu.VMEM((pairs, planes, 2 * LANES), F32),
            pltpu.VMEM((comps, pairs, 2 * planes, 2 * LANES), F32),
            pltpu.VMEM((comps, pairs, 2, planes, 2 * LANES), F32),
        ]
        + [pltpu.VMEM(piece, F32)] * 5
        + [
            facts,
            facts,
            pltpu.VMEM((per, 8, LANES), F32),
            pltpu.VMEM((8 * SUB, points), F32),
            pltpu.VMEM((16 * SUB, 4 * SUB), F32),
            pltpu.VMEM((8, 2 * half), F32),
        ]
        + [
            pltpu.SemaphoreType.DMA((2, comps, count)),
            pltpu.SemaphoreType.DMA((2, comps, count)),
            pltpu.SemaphoreType.DMA((2 * comps + 1,)),
            pltpu.SemaphoreType.DMA((2 * comps + 1,)),
        ],
        compiler_params=pltpu.CompilerParams(
            vmem_limit_bytes=60 * 1024 * 1024, collective_id=0, has_side_effects=True
        ),
        name="advect_and_solve",
    )(*operands)


def recover_nodes(mid, mine, other, side, kind_lanes, weight_lanes, recover_cols, rows):
    comps, count, points, _ = mid.shape
    half = mine.shape[2]
    per = LANES // rows
    nodes = count * per * points
    second_at = recover_cols.shape[0] // 2

    def kernel(mid_ref, mine_ref, other_ref, side_ref, kinds, factor, weights, out):
        second = side_ref[0:1] > 0.5
        bit = lax.broadcasted_iota(jnp.int32, (4 * SUB, LANES), 1) // 8 % 2 == 0
        tiles = []
        for tile in range(half // LANES):
            at = slice(tile * LANES, (tile + 1) * LANES)
            first_half = mine_ref[0, :, at]
            last_half = other_ref[0, :, at]
            low_rows = jnp.where(second, last_half, first_half)
            high_rows = jnp.where(second, first_half, last_half)
            tiles.append(jnp.where(bit, low_rows, pltpu.roll(high_rows, 8, 1)))
            tiles.append(jnp.where(bit, pltpu.roll(low_rows, LANES - 8, 1), high_rows))
        both = mm(stacked_weights(weights[...]), stacked_values(jnp.concatenate(tiles, axis=1)))
        found = jnp.where(kinds[0:1] > 0.5, both[second_at : second_at + points], both[:points])
        for part in range(count):
            at = slice(part * LANES, (part + 1) * LANES)
            block = mid_ref[0, part] * factor[0:1, at] + found[:, at]
            block = jnp.concatenate([block, jnp.zeros((LANES - points, LANES), F32)], axis=0).T
            for local in range(per):
                start = (part * per + local) * points
                out[0, :, start : start + points] = block[local * rows : (local + 1) * rows, :points]

    piece = pl.BlockSpec((1, 4 * SUB, half), lambda c: (c, 0, 0))
    extra = (side, kind_lanes, weight_lanes, recover_cols)
    return pl.pallas_call(
        kernel,
        grid=(comps,),
        in_specs=[pl.BlockSpec((1, count, points, LANES), lambda c: (c, 0, 0, 0)), piece, piece]
        + [whole_spec(item.shape) for item in extra],
        out_specs=pl.BlockSpec((1, rows, nodes), lambda c: (c, 0, 0)),
        out_shape=jax.ShapeDtypeStruct((comps, rows, nodes), F32),
        compiler_params=params(),
        name="recover_nodes",
    )(mid, mine, other, *extra)


def fast_device(
    velocity,
    geometry,
    element_kind,
    element_scale,
    dirichlet,
    schur_stiffness,
    schur_mass,
    lift,
    recover,
):
    count = lax.axis_size("planes")
    mid, mine, other, kinds, factor, recover_cols, side = advect_and_solve(
        velocity,
        geometry,
        element_kind[None],
        element_scale[None],
        dirichlet.swapaxes(0, 1),
        schur_stiffness.swapaxes(0, 1),
        schur_mass.swapaxes(0, 1),
        lift.swapaxes(0, 1),
        recover.transpose(2, 0, 1),
        count,
    )
    return recover_nodes(mid, mine, other, side, kinds, factor, recover_cols, velocity.shape[1])


def per_device(velocity, geometry, element_kind, *rest):
    count = lax.axis_size("planes")
    rows = velocity.shape[1]
    elems = element_kind.shape[0]
    fits = count & (count - 1) == 0 and rows == 16 and elems == LANES and elems * rows == count * LANES and lax.axis_size("elem") == 2
    body = fast_device if fits else plain_device
    return body(velocity, geometry, element_kind, *rest)


def solution(mesh):
    in_specs = (
        P(None, "planes", "elem"),
        P(None, "elem"),
        P("elem"),
        P("elem"),
        P(None, None, "elem"),
        P(),
        P(),
        P(),
        P(),
    )
    out_specs = P(None, "planes", "elem")
    return jax.shard_map(
        per_device, mesh=mesh, in_specs=in_specs, out_specs=out_specs, check_vma=False
    )
```

```python
import math

import jax
import jax.numpy as jnp
import numpy as np
from jax import lax
from jax.experimental import pallas as pl
from jax.experimental.pallas import tpu as pltpu
from jax.sharding import PartitionSpec as P

PLANES = 256
QUAD = 9
COLUMN_ELEMS = 32
CG_STEPS = 4


HIGHEST = lax.Precision.HIGHEST
SIGMA_COEF = 1.0
BETA_COEF = 0.01
STEP_DT = 0.002


def passed_along(value, axis, steps):
    count = lax.axis_size(axis)
    leading, last = (max(0, -steps), min(count, count - steps))
    return lax.ppermute(value, axis, [(source, source + steps) for source in range(leading, last)])


def gauss_derivative(points):
    nodes = -np.cos(np.pi * (2 * np.arange(points) + 1) / (2 * points))
    ident = np.eye(points)
    diffs = nodes[:, None] - nodes[None, :] + ident
    weights = 1.0 / np.prod(diffs, axis=1)
    matrix = weights[None, :] / weights[:, None] / diffs
    matrix = matrix * (1.0 - ident)
    return matrix - ident * matrix.sum(axis=1)[:, None]


def kron_tables():
    deriv = gauss_derivative(QUAD)
    identity = np.eye(QUAD)
    return (
        jnp.asarray(np.kron(deriv, identity), jnp.float32),
        jnp.asarray(np.kron(identity, deriv), jnp.float32),
    )


def fourier_tables(planes):
    zeta = jnp.arange(planes, dtype=jnp.int32)
    rows = jnp.arange(planes, dtype=jnp.int32)
    waves = (rows + 1) // 2
    phase = waves[None, :] * zeta[:, None] % planes
    angle = 2.0 * math.pi / planes * phase.astype(jnp.float32)
    cosine = jnp.cos(angle)
    sine = jnp.sin(angle)
    odd = (rows % 2 == 1)[None, :]
    first = (rows == 0)[None, :]
    last = (rows == planes - 1)[None, :]
    synth = jnp.where(first, 1.0, jnp.where(odd, cosine, sine))
    rate = BETA_COEF * waves.astype(jnp.float32)[None, :]
    slope = jnp.where(first | last, 0.0, jnp.where(odd, -rate * sine, rate * cosine))
    weight = jnp.where((rows == 0) | (rows == planes - 1), 1.0 / planes, 2.0 / planes).astype(
        jnp.float32
    )
    analysis = synth.T * weight[:, None]
    return (synth, slope, analysis)


def inner(first_pair, second_pair):
    return jnp.sum(first_pair[0] * second_pair[0], axis=(0, 2)) + jnp.sum(
        first_pair[1] * second_pair[1], axis=(0, 2)
    )


def global_total(first_pair, second_pair):
    return lax.psum(inner(first_pair, second_pair), "elem")


def global_squares(pair):
    return lax.psum(inner(pair, pair), "elem")


def assemble(outputs, incoming, free):
    left = outputs[:QUAD]
    right = outputs[QUAD : 2 * QUAD]
    bottom = outputs[2 * QUAD : 3 * QUAD]
    top = outputs[3 * QUAD :]
    vertical = left + jnp.concatenate([incoming, right[:, :, :-COLUMN_ELEMS]], axis=2)
    grid = top.reshape(top.shape[0], top.shape[1], -1, COLUMN_ELEMS)
    shifted = jnp.concatenate([jnp.zeros_like(grid[..., :1]), grid[..., :-1]], axis=3).reshape(
        bottom.shape
    )
    horizontal = bottom + shifted
    return (vertical * free[0], horizontal * free[1])


def plain_device(
    velocity,
    geometry,
    element_kind,
    element_scale,
    dirichlet,
    schur_stiffness,
    schur_mass,
    lift,
    recover,
):
    first, second = kron_tables()
    synth, slope, analysis = fourier_tables(PLANES)
    local_rows = velocity.shape[1]
    node_count = velocity.shape[2]
    share = node_count // lax.axis_size("planes")
    geo_part = lax.dynamic_slice_in_dim(geometry, lax.axis_index("planes") * share, share, 1)

    def transform(table, field):
        return jnp.einsum("zr,crm->czm", table, field, precision=HIGHEST)

    items = lax.all_to_all(velocity, "planes", split_axis=2, concat_axis=1, tiled=True)
    values = transform(synth, items)
    along_z = transform(slope, items)
    shaped = values.reshape(values.shape[:-1] + (-1, QUAD * QUAD))
    along_r = jnp.einsum("...en,mn->...em", shaped, first, precision=HIGHEST).reshape(values.shape)
    along_s = jnp.einsum("...en,mn->...em", shaped, second, precision=HIGHEST).reshape(values.shape)
    along_x = geo_part[0] * along_r + geo_part[1] * along_s
    along_y = geo_part[2] * along_r + geo_part[3] * along_s
    values, along_x, along_y, along_z = (values, along_x, along_y, along_z)
    advection = values[0] * along_x + values[1] * along_y + values[2] * along_z
    advection_hat = jnp.einsum("rz,czm->crm", analysis, advection, precision=HIGHEST)
    returned = lax.all_to_all(advection_hat, "planes", split_axis=1, concat_axis=2, tiled=True)
    intermediate = velocity - STEP_DT * returned
    elem_count = element_kind.shape[0]
    row_count = 3 * local_rows
    waves = (
        (lax.axis_index("planes") * local_rows + jnp.arange(local_rows, dtype=jnp.int32) + 1) // 2
    ).astype(jnp.float32)
    lam = jnp.tile(SIGMA_COEF + (BETA_COEF * waves) ** 2, 3)
    free = (1 - dirichlet).astype(jnp.float32)[:, :, None, :]
    chooser = (element_kind == 1).astype(jnp.float32)

    def element_apply(vector, kinds, scales):
        flat = vector.reshape(vector.shape[0], -1)
        results = []
        for kind in range(2):
            stiff = jnp.dot(schur_stiffness[kind], flat, precision=HIGHEST).reshape(vector.shape)
            massed = jnp.dot(schur_mass[kind], flat, precision=HIGHEST).reshape(vector.shape)
            results.append(stiff + lam[None, :, None] * massed)
        return scales[None, None, :] * jnp.where(kinds[None, None, :] > 0.5, results[1], results[0])

    def element_vector(vertical, horizontal):
        arriving = passed_along(vertical[:, :, :COLUMN_ELEMS], "elem", -1)
        right = jnp.concatenate([vertical[:, :, COLUMN_ELEMS:], arriving], axis=2)
        grid = horizontal.reshape(horizontal.shape[0], horizontal.shape[1], -1, COLUMN_ELEMS)
        top = jnp.concatenate([grid[..., 1:], jnp.zeros_like(grid[..., :1])], axis=3).reshape(
            horizontal.shape
        )
        return jnp.concatenate([vertical, right, horizontal, top], axis=0)

    node_values = (SIGMA_COEF * intermediate).reshape(row_count, elem_count, QUAD * QUAD)
    lifted = jnp.where(
        chooser[None, None, :] > 0.5,
        jnp.einsum("kn,ren->kre", lift[1], node_values, precision=HIGHEST),
        jnp.einsum("kn,ren->kre", lift[0], node_values, precision=HIGHEST),
    )
    lifted_right = passed_along(lifted[QUAD : 2 * QUAD, :, -COLUMN_ELEMS:], "elem", 1)
    forcing = assemble(lifted, lifted_right, free)
    trace = (jnp.zeros_like(forcing[0]), jnp.zeros_like(forcing[1]))
    residual = forcing
    direction = forcing
    norm_now = global_squares(residual)
    for sweep in range(CG_STEPS):
        outputs = element_apply(element_vector(direction[0], direction[1]), chooser, element_scale)
        operator_arriving = passed_along(outputs[QUAD : 2 * QUAD, :, -COLUMN_ELEMS:], "elem", 1)
        image = assemble(outputs, operator_arriving, free)
        alpha = (norm_now / global_total(direction, image))[None, :, None]
        trace = (trace[0] + alpha * direction[0], trace[1] + alpha * direction[1])
        residual = (residual[0] - alpha * image[0], residual[1] - alpha * image[1])
        norm_next = global_squares(residual)
        ratio = (norm_next / norm_now)[None, :, None]
        direction = (residual[0] + ratio * direction[0], residual[1] + ratio * direction[1])
        norm_now = norm_next
    vector = element_vector(trace[0], trace[1])
    recovered = jnp.where(
        chooser[None, :, None] > 0.5,
        jnp.einsum("nl,lre->ren", recover[1], vector, precision=HIGHEST),
        jnp.einsum("nl,lre->ren", recover[0], vector, precision=HIGHEST),
    )
    weight = SIGMA_COEF / (SIGMA_COEF + lam)
    result = (
        intermediate.reshape(row_count, elem_count, QUAD * QUAD) * weight[:, None, None] + recovered
    )
    return result.reshape(velocity.shape)


LANES = 128
SUB = 16
F32 = jnp.float32
BF16 = jnp.bfloat16


def split(value):
    high = value.astype(BF16)
    return high, (value - high.astype(F32)).astype(BF16)


def np_split(value):
    high = np.asarray(value, np.float32).astype(BF16)
    low = (np.asarray(value, np.float64) - high.astype(np.float64)).astype(np.float32).astype(BF16)
    return high, low


def mm(first, second):
    return jnp.dot(first, second, preferred_element_type=F32)


def stacked_weights(weights):
    high, low = split(weights)
    return jnp.concatenate([high, high, low], axis=1)


def stacked_values(values):
    high, low = split(values)
    return jnp.concatenate([high, low, high], axis=0)


def advect_tables(planes):
    zeta = np.arange(planes)
    rows = np.arange(planes)
    waves = (rows + 1) // 2
    angle = 2.0 * np.pi / planes * ((waves[None, :] * zeta[:, None]) % planes)
    odd = (rows % 2 == 1)[None, :]
    first = (rows == 0)[None, :]
    last = (rows == planes - 1)[None, :]
    synth = np.where(first, 1.0, np.where(odd, np.cos(angle), np.sin(angle)))
    rate = BETA_COEF * waves[None, :]
    slope = np.where(first | last, 0.0, np.where(odd, -rate * np.sin(angle), rate * np.cos(angle)))
    weight = np.where((rows == 0) | (rows == planes - 1), 1.0 / planes, 2.0 / planes)
    analysis = synth.T * weight[:, None]
    high, low = np_split(np.concatenate([synth, slope], axis=0))
    forward = np.concatenate([high, high, low], axis=1)
    high, low = np_split(analysis)
    backward = np.concatenate([high, high, low], axis=1)
    points = QUAD * QUAD
    deriv = gauss_derivative(QUAD)
    both = np.zeros((LANES, 2 * LANES))
    both[:points, :points] = np.kron(deriv, np.eye(QUAD)).T
    both[:points, LANES : LANES + points] = np.kron(np.eye(QUAD), deriv).T
    high, low = np_split(both)
    return jnp.asarray(forward), jnp.asarray(backward), jnp.asarray(np.concatenate([high, high, low], axis=0))


def whole_spec(shape):
    return pl.BlockSpec(shape, lambda *_: (0,) * len(shape))


def params():
    return pltpu.CompilerParams(vmem_limit_bytes=60 * 1024 * 1024)


def solve_rows(own, other, own_fact, other_fact, lam, side_row, weights):
    half = own.shape[1]
    wide = 2 * half
    column = COLUMN_ELEMS // SUB * LANES
    second = jnp.concatenate([side_row] * (half // LANES), axis=1) > 0.5

    def joined(first, last):
        return jnp.concatenate([jnp.where(second, last, first), jnp.where(second, first, last)], axis=1)

    facts = joined(own_fact, other_fact)
    free_v = facts[:SUB]
    free_h = facts[SUB : 2 * SUB]
    is_second = facts[2 * SUB : 2 * SUB + 1] > 0.5
    scale = facts[2 * SUB + 1 : 2 * SUB + 2]
    w_all = stacked_weights(weights)
    lane = lax.broadcasted_iota(jnp.int32, (1, wide), 1)
    along = lane % LANES // SUB
    odd_half = lane // 8 % 2 == 1
    tile = lane // LANES
    per_column = COLUMN_ELEMS // SUB
    top_edge = (tile % per_column == per_column - 1) & odd_half & (along == SUB // 2 - 1)
    low_edge = (tile % per_column == 0) & jnp.logical_not(odd_half) & (along == 0)

    def above(x):
        last = jnp.where(odd_half, pltpu.roll(x, wide - 8, 1), pltpu.roll(x, 104, 1))
        moved = jnp.where(along < SUB // 2 - 1, pltpu.roll(x, wide - 16, 1), last)
        return jnp.where(top_edge, 0.0, moved)

    def below(x):
        head = jnp.where(odd_half, pltpu.roll(x, wide - 104, 1), pltpu.roll(x, 8, 1))
        moved = jnp.where(along > 0, pltpu.roll(x, 16, 1), head)
        return jnp.where(low_edge, 0.0, moved)

    edge = jnp.zeros((SUB, column), F32)

    def vector_of(v, h):
        right = jnp.concatenate([v[:, column:], edge], axis=1)
        return jnp.concatenate([v, right, h, above(h)], axis=0)

    def gather(parts):
        right = jnp.concatenate([edge, parts[SUB : 2 * SUB, :-column]], axis=1)
        v = (parts[:SUB] + right) * free_v
        h = (parts[2 * SUB : 3 * SUB] + below(parts[3 * SUB :])) * free_h
        return v, h

    def total(product):
        acc = product[:, :LANES]
        for at in range(1, wide // LANES):
            acc = acc + product[:, at * LANES : (at + 1) * LANES]
        acc = jnp.sum(acc, axis=0, keepdims=True)
        acc = jnp.broadcast_to(acc, (8, LANES))
        for step in (8, 16, 32, 64):
            acc = acc + pltpu.roll(acc, step, 1)
        return acc[0:1]

    def spread(row):
        return jnp.concatenate([row] * (wide // LANES), axis=1)

    res_v, res_h = gather(joined(own, other))
    now = total(res_v * res_v + res_h * res_h)
    zero = jnp.zeros_like(res_v)

    def sweep(_, state):
        tr_v, tr_h, res_v, res_h, dir_v, dir_h, now = state
        both = mm(w_all, stacked_values(vector_of(dir_v, dir_h)))
        rows = 4 * SUB
        stiff = jnp.where(is_second, both[rows : 2 * rows], both[:rows])
        mass = jnp.where(is_second, both[3 * rows :], both[2 * rows : 3 * rows])
        im_v, im_h = gather(scale * (stiff + lam * mass))
        alpha = spread(now / total(dir_v * im_v + dir_h * im_h))
        tr_v, tr_h = tr_v + alpha * dir_v, tr_h + alpha * dir_h
        res_v, res_h = res_v - alpha * im_v, res_h - alpha * im_h
        fresh = total(res_v * res_v + res_h * res_h)
        ratio = spread(fresh / now)
        return tr_v, tr_h, res_v, res_h, res_v + ratio * dir_v, res_h + ratio * dir_h, fresh

    state = lax.fori_loop(0, CG_STEPS, sweep, (zero, zero, res_v, res_h, res_v, res_h, now))
    vector = vector_of(state[0], state[1])
    mine = jnp.where(second, vector[:, half:], vector[:, :half])
    away = jnp.where(second, vector[:, :half], vector[:, half:])
    return mine, away


def exact(first, second):
    return jnp.dot(first, second, precision=HIGHEST, preferred_element_type=F32)


def iota(shape, axis):
    return lax.broadcasted_iota(jnp.int32, shape, axis)


def lam_of(row):
    return SIGMA_COEF + (BETA_COEF * ((row + 1) // 2).astype(F32)) ** 2


def advect_and_solve(velocity, geometry, kind, scale, dirichlet, stiffness, mass, lift_maps, recover_maps, count):
    elems = kind.shape[1]
    comps, rows, nodes = velocity.shape
    points = QUAD * QUAD
    per = LANES // rows
    pairs = per // 2
    planes = count * rows
    half = count * LANES // 2
    forward, backward, deriv = advect_tables(planes)

    def kernel(
        vel_ref, geo_ref, kind_ref, scale_ref, fixed_ref, stiff_ref, mass_ref, lift_in, recover_in,
        forward_ref, backward_ref, deriv_ref,
        out,
        mid, mine, kinds, factor, recover_out, side_ref,
        sent, recv, hats, ret, store, fields, slopes, own, away, other, traces, their_traces, facts_out, their_facts,
        geo, lift_ref, mat_ref, lam_ref,
        send_sem, recv_sem, pair_send, pair_recv,
    ):
        me = lax.axis_index("planes")
        core = lax.axis_index("elem")
        barrier = pltpu.get_barrier_semaphore()

        def peer_at(step):
            bits = count.bit_length() - 1
            peer = 0
            for bit in range(bits):
                weight = count // 2 // 2**bit
                peer = peer + weight * ((me // weight + step // 2**bit) % 2)
            return peer

        def greet(step, carry):
            pl.semaphore_signal(
                barrier, inc=1, device_id={"planes": peer_at(step)}, device_id_type=pl.DeviceIdType.MESH
            )
            return carry

        lax.fori_loop(1, count, greet, 0)
        pl.semaphore_signal(barrier, inc=1, device_id={"elem": 1 - core}, device_id_type=pl.DeviceIdType.MESH)

        def copy_to(source, target, way, comp, peer):
            return pltpu.make_async_remote_copy(
                src_ref=source.at[comp, peer],
                dst_ref=target.at[comp, me],
                send_sem=send_sem.at[way, comp, peer],
                recv_sem=recv_sem.at[way, comp, me],
                device_id={"planes": peer},
                device_id_type=pl.DeviceIdType.MESH,
            )

        def copy_from(source, target, way, comp, peer):
            return pltpu.make_async_remote_copy(
                src_ref=source.at[comp, peer],
                dst_ref=target.at[comp, peer],
                send_sem=send_sem.at[way, comp, peer],
                recv_sem=recv_sem.at[way, comp, peer],
                device_id={"planes": peer},
                device_id_type=pl.DeviceIdType.MESH,
            )

        def start_all(source, target, way, comp):
            def one(step, carry):
                copy_to(source, target, way, comp, peer_at(step)).start()
                return carry

            lax.fori_loop(1, count, one, 0)

        def pair_copy(source, target, at):
            return pltpu.make_async_remote_copy(
                src_ref=source,
                dst_ref=target,
                send_sem=pair_send.at[at],
                recv_sem=pair_recv.at[at],
                device_id={"elem": 1 - core},
                device_id_type=pl.DeviceIdType.MESH,
            )

        def pack(comp):
            for part in range(count):
                pieces = []
                for local in range(per):
                    at = (part * per + local) * points
                    pieces.append(vel_ref[comp, :, at : at + points])
                sent[comp, part] = jnp.concatenate(pieces, axis=0).T

        def arrive(comp, part, block):
            block = jnp.concatenate([block, jnp.zeros((LANES - points, LANES), F32)], axis=0).T
            for local in range(per):
                at = local % 2 * LANES
                store[local // 2, pl.ds(pl.multiple_of(part * rows, rows), rows), at : at + LANES] = block[
                    local * rows : (local + 1) * rows
                ]

        def arrive_all(comp):
            arrive(comp, me, sent[comp, me])

            def one(step, carry):
                part = peer_at(step)
                copy_from(sent, recv, 0, comp, part).wait_recv()
                arrive(comp, part, recv[comp, part])
                return carry

            lax.fori_loop(1, count, one, 0)

        def synthesize(comp):
            def one(pair, carry):
                fields[comp, pair] = mm(forward_ref[...], stacked_values(store[pair]))
                return carry

            lax.fori_loop(0, pairs, one, 0)

        def derive(comp):
            def one(pair, carry):
                for which in range(2):
                    high, low = split(fields[comp, pair, :planes, which * LANES : (which + 1) * LANES])
                    slopes[comp, pair, which] = mm(jnp.concatenate([high, low], axis=1), deriv_ref[: 2 * LANES]) + mm(
                        high, deriv_ref[2 * LANES :]
                    )
                return carry

            lax.fori_loop(0, pairs, one, 0)

        def advect(comp):
            def one(pair, carry):
                results = []
                for which in range(2):
                    at = slice(which * LANES, (which + 1) * LANES)
                    vel = [fields[item, pair, :planes, at] for item in range(comps)]
                    part = geo[pair * 2 + which]
                    results.append(
                        slopes[comp, pair, which, :, :LANES] * (vel[0] * part[0:1] + vel[1] * part[2:3])
                        + slopes[comp, pair, which, :, LANES:] * (vel[0] * part[1:2] + vel[1] * part[3:4])
                        + vel[2] * fields[comp, pair, planes:, at]
                    )
                store[pair] = mm(backward_ref[...], stacked_values(jnp.concatenate(results, axis=1)))
                return carry

            lax.fori_loop(0, pairs, one, 0)
            for part in range(count):
                block = jnp.concatenate(
                    [
                        store[local // 2, part * rows : (part + 1) * rows, local % 2 * LANES : (local % 2 + 1) * LANES]
                        for local in range(per)
                    ],
                    axis=0,
                )
                hats[comp, part] = block.T[:points]

        def lift(comp):
            def one(step, carry):
                copy_from(hats, ret, 1, comp, peer_at(step)).wait_recv()
                return carry

            lax.fori_loop(1, count, one, 0)
            ret[comp, me] = hats[comp, me]
            for part in range(count):
                mid[comp, part] = sent[comp, part] - STEP_DT * ret[comp, part]
            field = jnp.concatenate([mid[comp, part] for part in range(count)], axis=1)
            high, low = split(SIGMA_COEF * field)
            w_high, w_low = split(lift_ref[...])
            both = mm(w_high, high) + (mm(w_high, low) + mm(w_low, high))
            lifted = jnp.where(kinds[0:1] > 0.5, both[4 * SUB :], both[: 4 * SUB])
            bit = lax.broadcasted_iota(jnp.int32, (4 * SUB, LANES), 1) // 8 % 2 == 0
            second = side_ref[0:1] > 0.5
            for tile in range(count // 2):
                even = lifted[:, 2 * tile * LANES : (2 * tile + 1) * LANES]
                odd = lifted[:, (2 * tile + 1) * LANES : (2 * tile + 2) * LANES]
                low_rows = jnp.where(bit, even, pltpu.roll(odd, 8, 1))
                high_rows = jnp.where(bit, pltpu.roll(even, LANES - 8, 1), odd)
                at = slice(tile * LANES, (tile + 1) * LANES)
                own[comp, :, at] = jnp.where(second, high_rows, low_rows)
                away[comp, :, at] = jnp.where(second, low_rows, high_rows)
            pair_copy(away.at[comp], other.at[comp], comp).start()

        def solve(comp):
            pair_copy(away.at[comp], other.at[comp], comp).wait_recv()
            kept, theirs = solve_rows(
                own[comp], other[comp], facts_out[...], their_facts[...], lam_ref[0:1], side_ref[0:1], mat_ref[...]
            )
            mine[comp] = kept
            traces[comp] = theirs
            pair_copy(traces.at[comp], their_traces.at[comp], comps + comp).start()

        def recover(comp):
            pair_copy(traces.at[comp], their_traces.at[comp], comps + comp).wait_recv()
            second = side_ref[0:1] > 0.5
            bit = lax.broadcasted_iota(jnp.int32, (4 * SUB, LANES), 1) // 8 % 2 == 0
            tiles = []
            for tile in range(half // LANES):
                at = slice(tile * LANES, (tile + 1) * LANES)
                first_half = mine[comp, :, at]
                last_half = their_traces[comp, :, at]
                low_rows = jnp.where(second, last_half, first_half)
                high_rows = jnp.where(second, first_half, last_half)
                tiles.append(jnp.where(bit, low_rows, pltpu.roll(high_rows, 8, 1)))
                tiles.append(jnp.where(bit, pltpu.roll(low_rows, LANES - 8, 1), high_rows))
            both = mm(stacked_weights(recover_out[...]), stacked_values(jnp.concatenate(tiles, axis=1)))
            found = jnp.where(kinds[0:1] > 0.5, both[88 : 88 + points], both[:points])
            for part in range(count):
                at = slice(part * LANES, (part + 1) * LANES)
                block = mid[comp, part] * factor[0:1, at] + found[:, at]
                block = jnp.concatenate([block, jnp.zeros((LANES - points, LANES), F32)], axis=0).T
                for local in range(per):
                    start = (part * per + local) * points
                    out[comp, :, start : start + points] = block[local * rows : (local + 1) * rows, :points]

        def prepare():
            group = iota((4 * SUB, 4 * QUAD), 0)
            place = group // SUB * QUAD + group % SUB
            widen = ((place == iota((4 * SUB, 4 * QUAD), 1)) & (group % SUB < QUAD)).astype(F32)
            group = iota((4 * QUAD, 4 * SUB), 1)
            place = group // SUB * QUAD + group % SUB
            widen_cols = ((place == iota((4 * QUAD, 4 * SUB), 0)) & (group % SUB < QUAD)).astype(F32)
            recover_out[...] = jnp.zeros_like(recover_out)
            for which in range(2):
                at = which * 4 * SUB
                mat_ref[at : at + 4 * SUB] = exact(exact(widen, stiff_ref[:, which, :]), widen_cols)
                at = at + 8 * SUB
                mat_ref[at : at + 4 * SUB] = exact(exact(widen, mass_ref[:, which, :]), widen_cols)
                lift_ref[which * 4 * SUB : (which + 1) * 4 * SUB] = exact(widen, lift_in[:, which, :])
                recover_out[which * 88 : which * 88 + points] = exact(widen, recover_in[:, which, :]).T
            is_second = (kind_ref[...] == 1).astype(F32)
            pad = jnp.zeros((SUB - QUAD, elems), F32)
            free_v = (1 - fixed_ref[:, 0, :]).astype(F32)
            free_h = (1 - fixed_ref[:, 1, :]).astype(F32)
            table = jnp.concatenate(
                [free_v, pad, free_h, pad, is_second, scale_ref[...], jnp.zeros((6, elems), F32)], axis=0
            )
            lane = iota((elems, half), 1)
            element = lane // LANES * 16 + lane // 8 % 2 * 8 + lane % LANES // 16
            facts_out[...] = exact(table, (element == iota((elems, half), 0)).astype(F32))
            lane = iota((elems, 2 * half), 1)
            spread = (lane // rows == iota((elems, 2 * half), 0)).astype(F32)
            kinds[...] = exact(jnp.broadcast_to(is_second, (8, elems)), spread)
            lane = iota((8, 2 * half), 1)
            lam_ref[...] = lam_of(me * rows + core * 8 + lane % 8)
            factor[...] = SIGMA_COEF / (SIGMA_COEF + lam_of(me * rows + lane % rows))
            side_ref[...] = jnp.full((8, LANES), core, jnp.int32).astype(F32)
            geo[...] = jnp.zeros_like(geo)
            for part in range(count):

                @pl.when(me == part)
                def _():
                    for local in range(per):
                        at = (part * per + local) * points
                        geo[local, 0:4, 0:points] = geo_ref[:, at : at + points]

        pack(0)
        pl.semaphore_wait(barrier, count)
        start_all(sent, recv, 0, 0)
        for comp in range(1, comps):
            pack(comp)
            start_all(sent, recv, 0, comp)
        prepare()
        pair_copy(facts_out, their_facts, 2 * comps).start()
        for comp in range(comps):
            arrive_all(comp)
            synthesize(comp)
            if comp < comps - 1:
                derive(comp)
        for comp in range(comps):
            if comp == comps - 1:
                derive(comp)
            advect(comp)
            start_all(hats, ret, 1, comp)
        pair_copy(facts_out, their_facts, 2 * comps).wait_recv()
        for comp in range(comps):
            lift(comp)
            if comp > 0:
                recover(comp - 1)
            solve(comp)
        recover(comps - 1)
        pair_copy(facts_out, their_facts, 2 * comps).wait_send()
        for comp in range(comps):
            pair_copy(away.at[comp], other.at[comp], comp).wait_send()
            pair_copy(traces.at[comp], their_traces.at[comp], comps + comp).wait_send()

            def drain(step, carry):
                peer = peer_at(step)
                copy_to(sent, recv, 0, comp, peer).wait_send()
                copy_to(hats, ret, 1, comp, peer).wait_send()
                return carry

            lax.fori_loop(1, count, drain, 0)

    message = (comps, count, points, LANES)
    piece = (comps, 4 * SUB, half)
    operands = (velocity, geometry, kind, scale, dirichlet, stiffness, mass, lift_maps, recover_maps)
    operands = operands + (forward, backward, deriv)
    facts = pltpu.VMEM((40, half), F32)
    vmem = pl.BlockSpec(memory_space=pltpu.VMEM)
    return pl.pallas_call(
        kernel,
        in_specs=[vmem] * len(operands),
        out_specs=vmem,
        out_shape=jax.ShapeDtypeStruct(velocity.shape, F32),
        scratch_shapes=[
            pltpu.VMEM(message, F32),
            pltpu.VMEM(piece, F32),
            pltpu.VMEM((8, 2 * half), F32),
            pltpu.VMEM((8, 2 * half), F32),
            pltpu.VMEM((2 * 88, 4 * SUB), F32),
            pltpu.VMEM((8, LANES), F32),
        ]
        + [pltpu.VMEM(message, F32)] * 4
        + [
            pltpu.VMEM((pairs, planes, 2 * LANES), F32),
            pltpu.VMEM((comps, pairs, 2 * planes, 2 * LANES), F32),
            pltpu.VMEM((comps, pairs, 2, planes, 2 * LANES), F32),
        ]
        + [pltpu.VMEM(piece, F32)] * 5
        + [
            facts,
            facts,
            pltpu.VMEM((per, 8, LANES), F32),
            pltpu.VMEM((8 * SUB, points), F32),
            pltpu.VMEM((16 * SUB, 4 * SUB), F32),
            pltpu.VMEM((8, 2 * half), F32),
        ]
        + [
            pltpu.SemaphoreType.DMA((2, comps, count)),
            pltpu.SemaphoreType.DMA((2, comps, count)),
            pltpu.SemaphoreType.DMA((2 * comps + 1,)),
            pltpu.SemaphoreType.DMA((2 * comps + 1,)),
        ],
        compiler_params=pltpu.CompilerParams(
            vmem_limit_bytes=60 * 1024 * 1024, collective_id=0, has_side_effects=True
        ),
        name="advect_and_solve",
    )(*operands)


def fast_device(
    velocity,
    geometry,
    element_kind,
    element_scale,
    dirichlet,
    schur_stiffness,
    schur_mass,
    lift,
    recover,
):
    count = lax.axis_size("planes")
    return advect_and_solve(
        velocity,
        geometry,
        element_kind[None],
        element_scale[None],
        dirichlet.swapaxes(0, 1),
        schur_stiffness.swapaxes(0, 1),
        schur_mass.swapaxes(0, 1),
        lift.swapaxes(0, 1),
        recover.transpose(2, 0, 1),
        count,
    )


def per_device(velocity, geometry, element_kind, *rest):
    count = lax.axis_size("planes")
    rows = velocity.shape[1]
    elems = element_kind.shape[0]
    fits = count & (count - 1) == 0 and rows == 16 and elems == LANES and elems * rows == count * LANES and lax.axis_size("elem") == 2
    body = fast_device if fits else plain_device
    return body(velocity, geometry, element_kind, *rest)


def solution(mesh):
    in_specs = (
        P(None, "planes", "elem"),
        P(None, "elem"),
        P("elem"),
        P("elem"),
        P(None, None, "elem"),
        P(),
        P(),
        P(),
        P(),
    )
    out_specs = P(None, "planes", "elem")
    return jax.shard_map(
        per_device, mesh=mesh, in_specs=in_specs, out_specs=out_specs, check_vma=False
    )
```
